512 devices in a mesh: pix: 64 (over z, y), mode: 8 (over x, core).
Axes of the slice: x: 4, y: 8, z: 8, core: 2. Of those that a mesh axis runs over, the one named last changes fastest.
Arguments:
- frames: bfloat16 [4, 32768, 2048], P(None, 'pix', 'mode'), may hold values from 0 to 4
- ref_pixels: int32 [64], replicated, may hold values from 0 to 32767
Outputs:
- gram_band: float32 [2, 2048, 1024], P(None, 'mode', 'pix')
- gram_diag: float32 [2, 2048, 256], P(None, 'mode', 'pix')
The draws below stay inside these ranges and needn't reach their ends.
Inputs may be any that keep to these rules, and one draw needn't show every extreme that they name: `ref_pixels`: indices of reference pixels; an index may appear more than once.
All inputs are finite; a program needn't handle non-finite values.
Results may differ from the reference program's by a relative error of at most 0.0088.
Values may be sent and summed in bfloat16 or wider, within the bound.
No kernel may reach another device: no remote copies, remote signals or barrier semaphores. Data moves between devices by JAX's collectives and lax.ppermute only.
A program may use at most 64 MiB of HBM per device.

```python
import math
import jax
import jax.numpy as jnp
from jax import lax

MODES = 2048
NREF = 64
PIXELS = 32768
N_MODE = 8


def plant(values, rng, least, largest):
    longest = values.shape.index(max(values.shape))
    spots = []
    for shift in (0, 1):
        where = [jax.random.randint(jax.random.fold_in(rng, axis), (), 0, length) for axis, length in enumerate(values.shape)]
        where[longest] = (where[longest] + shift) % values.shape[longest]
        spots.append(tuple(where))
    return values.at[spots[0]].set(least).at[spots[1]].set(largest)


def block_scale(stream_key, shape, shards, smallest, largest):
    gain, own = 1.0, jax.random.fold_in(stream_key, 6)
    for axis_at, parts in shards:
        heights = jnp.exp(jax.random.uniform(jax.random.fold_in(own, axis_at), (parts,), jnp.float32, smallest / len(shards), largest / len(shards)))
        gain = gain * jnp.repeat(heights, shape[axis_at] // parts).reshape([-1 if axis == axis_at else 1 for axis in range(len(shape))])
    return gain


def setup_inputs(seed: int = 0) -> dict:
    streams_of = jax.random.split(jax.random.key(seed), 3)
    frames = jnp.clip(4.0 * jax.random.uniform(streams_of[0], (4, PIXELS, MODES), jnp.float32) ** block_scale(streams_of[0], (4, PIXELS, MODES), ((1, 64), (2, 8)), -0.2, 0.2), 0.0, 4.0).astype(jnp.bfloat16)
    ref_pixels = plant(jax.random.randint(streams_of[1], (NREF,), 0, PIXELS), jax.random.fold_in(streams_of[1], 1), 0, PIXELS - 1).astype(jnp.int32)
    return dict(frames=frames, ref_pixels=ref_pixels)


def reference(frames, ref_pixels):
    frame_float = frames.astype(jnp.float32)
    real_part = (frame_float[0] - frame_float[2]).astype(jnp.bfloat16)
    imag_part = (frame_float[3] - frame_float[1]).astype(jnp.bfloat16)
    ref_real = lax.optimization_barrier(jnp.sum(jnp.take(real_part, ref_pixels, axis=0).astype(jnp.float32), axis=0))
    ref_imag = lax.optimization_barrier(jnp.sum(jnp.take(imag_part, ref_pixels, axis=0).astype(jnp.float32), axis=0))
    magnitude = jnp.maximum(jnp.sqrt(ref_real * ref_real + ref_imag * ref_imag), 1.0)
    phase_real = ref_real / magnitude
    phase_imag = ref_imag / magnitude
    stacked = jnp.concatenate([real_part, imag_part], axis=0)
    turned = jnp.concatenate([imag_part, -real_part], axis=0)
    block_width = MODES // N_MODE
    full_width = (N_MODE // 2 + 1) * block_width
    stacked_twice = jnp.concatenate([stacked, stacked], axis=1)
    turned_twice = jnp.concatenate([turned, turned], axis=1)
    twice_real = jnp.concatenate([phase_real, phase_real], axis=0)
    twice_imag = jnp.concatenate([phase_imag, phase_imag], axis=0)
    pixel_scale = 1.0 / math.sqrt(PIXELS)

    def one_block(block_index):
        offset = (block_index * block_width).astype(jnp.int32)
        row_fields = lax.dynamic_slice_in_dim(stacked, offset, block_width, 1)
        col_fields = lax.dynamic_slice_in_dim(stacked_twice, offset, full_width, 1)
        turned_cols = lax.dynamic_slice_in_dim(turned_twice, offset, full_width, 1)
        gram_real = jnp.dot(row_fields.T, col_fields, preferred_element_type=jnp.float32)
        gram_imag = jnp.dot(row_fields.T, turned_cols, preferred_element_type=jnp.float32)
        row_real = lax.dynamic_slice_in_dim(phase_real, offset, block_width, 0)[:, None]
        row_imag = lax.dynamic_slice_in_dim(phase_imag, offset, block_width, 0)[:, None]
        col_real = lax.dynamic_slice_in_dim(twice_real, offset, full_width, 0)[None, :]
        col_imag = lax.dynamic_slice_in_dim(twice_imag, offset, full_width, 0)[None, :]
        unit_real = row_real * col_real + row_imag * col_imag
        unit_imag = row_imag * col_real - row_real * col_imag
        return jnp.stack([(unit_real * gram_real - unit_imag * gram_imag) * pixel_scale, (unit_real * gram_imag + unit_imag * gram_real) * pixel_scale])
    full_tiles = lax.map(one_block, jnp.arange(N_MODE, dtype=jnp.int32))
    full_rows = jnp.transpose(full_tiles, (1, 0, 2, 3)).reshape(2, MODES, full_width)
    return (full_rows[:, :, block_width:], full_rows[:, :, :block_width])
```

```python
import math

import jax
import jax.numpy as jnp
from jax import lax
from jax.experimental import pallas as pl
from jax.experimental.pallas import tpu as pltpu
from jax.sharding import PartitionSpec as P

BF16 = jnp.bfloat16
F32 = jnp.float32
VMEM = pl.BlockSpec(memory_space=pltpu.VMEM)
SMEM = pl.BlockSpec(memory_space=pltpu.SMEM)
REF_ROWS = 8


def cost(flops, nbytes):
    return pl.CostEstimate(flops=flops, bytes_accessed=nbytes, transcendentals=0)


def dot_pixels(cols, rows):
    return lax.dot_general(cols, rows, (((0,), (0,)), ((), ())), preferred_element_type=F32)


def gram_t(col_real, col_imag, row_real, row_imag, row_imag_neg):
    real = dot_pixels(col_real, row_real) + dot_pixels(col_imag, row_imag)
    imag = dot_pixels(col_imag, row_real) + dot_pixels(col_real, row_imag_neg)
    return real, imag


def fields_kernel(frames_ref, fields_ref):
    fields_ref[0] = (frames_ref[0].astype(F32) - frames_ref[2].astype(F32)).astype(BF16)
    fields_ref[1] = (frames_ref[3].astype(F32) - frames_ref[1].astype(F32)).astype(BF16)


def early_kernel(base_ref, fields_ref, pixels_ref, out_ref):
    dests, slot_rows, width = out_ref.shape
    diag_cols = width // dests
    real, imag = fields_ref[0], fields_ref[1]
    positions = base_ref[0] + lax.broadcasted_iota(jnp.int32, (pixels_ref.shape[0], real.shape[0]), 1)
    counts = jnp.sum((pixels_ref[...] == positions).astype(F32), axis=0, keepdims=True)
    counts = jnp.broadcast_to(counts, (8, real.shape[0])).astype(BF16)
    ref_real = jnp.dot(counts, real, preferred_element_type=F32)
    ref_imag = jnp.dot(counts, imag, preferred_element_type=F32)
    row = lax.broadcasted_iota(jnp.int32, ref_real.shape, 0)
    high_real = ref_real.astype(BF16).astype(F32)
    high_imag = ref_imag.astype(BF16).astype(F32)
    refs = jnp.where(row == 0, high_real, ref_real - high_real)
    refs = jnp.where(row == 2, high_imag, refs)
    refs = jnp.where(row == 3, ref_imag - high_imag, refs)
    refs = jnp.where(row > 3, 0.0, refs)
    diag_real, diag_imag = gram_t(real, imag, real, imag, -imag)
    rows = jnp.concatenate(
        [diag_real, diag_imag, refs, jnp.zeros((128 - refs.shape[0], width), F32)], axis=0
    ).astype(BF16)
    slot_at = lax.broadcasted_iota(jnp.int32, (dests * slot_rows, rows.shape[0]), 0)
    source = lax.broadcasted_iota(jnp.int32, (dests * slot_rows, rows.shape[0]), 1)
    dest, slot = slot_at // slot_rows, slot_at % slot_rows
    diag_source = (slot // diag_cols) * width + dest * diag_cols + slot % diag_cols
    wanted = jnp.where(slot < 2 * diag_cols, diag_source, 2 * width + slot - 2 * diag_cols)
    pick = jnp.where(wanted == source, 1.0, 0.0).astype(BF16)
    placed = jnp.dot(pick, rows, preferred_element_type=F32)
    out_ref[...] = placed.reshape(dests, slot_rows, width).astype(BF16)


def band_kernel(own_ref, one_ref, two_ref, three_ref, four_ref, out_ref):
    row_real, row_imag = own_ref[0], own_ref[1]
    row_imag_neg = -row_imag
    width = row_real.shape[1]
    part_cols = out_ref.shape[1] // 2
    tile_dests = width // part_cols
    for at, block in enumerate((one_ref, two_ref, three_ref, four_ref)):
        real, imag = gram_t(block[0], block[1], row_real, row_imag, row_imag_neg)
        dests = pl.ds(at * tile_dests, tile_dests)
        out_ref[dests, :part_cols, :] = real.reshape(tile_dests, part_cols, width).astype(BF16)
        out_ref[dests, part_cols:, :] = imag.reshape(tile_dests, part_cols, width).astype(BF16)


def unit_phase(real, imag):
    magnitude = jnp.maximum(jnp.sqrt(real * real + imag * imag), 1.0)
    return real / magnitude, imag / magnitude


def pick_lanes(values, start, count):
    lanes = values.shape[1]
    lane = lax.broadcasted_iota(jnp.int32, (count, lanes), 1)
    row = lax.broadcasted_iota(jnp.int32, (count, lanes), 0)
    return jnp.sum(jnp.where(lane == start + row, values, 0.0), axis=1, keepdims=True)


def rotate(real, imag, row_phase, col_phase, pixel_scale):
    unit_real = row_phase[0] * col_phase[0] + row_phase[1] * col_phase[1]
    unit_imag = row_phase[1] * col_phase[0] - row_phase[0] * col_phase[1]
    return (
        (unit_real * real - unit_imag * imag) * pixel_scale,
        (unit_real * imag + unit_imag * real) * pixel_scale,
    )


def final_kernel(pixel_scale, starts_ref, early_ref, own_ref, other_ref, band_ref, band_out, diag_out):
    part_cols, diag_cols = band_out.shape[1], diag_out.shape[1]
    band = jnp.sum(band_ref[...].astype(F32), axis=0)
    diag = jnp.sum(early_ref[...].astype(F32), axis=0)[: 2 * diag_cols]
    row_phase = unit_phase(own_ref[0:1, :], own_ref[1:2, :])
    other_phase = unit_phase(other_ref[0:1, :], other_ref[1:2, :])
    col_phase = [pick_lanes(part, starts_ref[0], part_cols) for part in other_phase]
    band_out[0], band_out[1] = rotate(band[:part_cols], band[part_cols:], row_phase, col_phase, pixel_scale)
    diag_phase = [pick_lanes(part, starts_ref[1], diag_cols) for part in row_phase]
    diag_out[0], diag_out[1] = rotate(diag[:diag_cols], diag[diag_cols:], row_phase, diag_phase, pixel_scale)


def shards(frames, ref_pixels):
    pix_count = lax.axis_size("pix")
    mode_count = lax.axis_size("mode")
    pix_index = lax.axis_index("pix")
    mode_index = lax.axis_index("mode")
    pixel_rows, width = frames.shape[1:]
    tiles = mode_count // 2
    tile_dests = pix_count // tiles
    part_cols = width // tile_dests
    diag_cols = width // pix_count
    slot_rows = 2 * diag_cols + REF_ROWS
    field_bytes = 2 * pixel_rows * width * 2
    tile_flops = 8 * pixel_rows * width * width

    def shift(array, step):
        pairs = [((m + step) % mode_count, m) for m in range(mode_count)]
        return lax.ppermute(array, "mode", pairs)

    def swap(array):
        return lax.ppermute(array, "mode", [(m ^ 1, m) for m in range(mode_count)])

    fields = pl.pallas_call(
        fields_kernel,
        out_shape=jax.ShapeDtypeStruct((2, pixel_rows, width), BF16),
        in_specs=[VMEM],
        out_specs=VMEM,
        cost_estimate=cost(4 * pixel_rows * width, 3 * field_bytes),
    )(frames)
    two = shift(fields, 2)
    four = shift(fields, 4)

    early = pl.pallas_call(
        early_kernel,
        out_shape=jax.ShapeDtypeStruct((pix_count, slot_rows, width), BF16),
        in_specs=[SMEM, VMEM, VMEM],
        out_specs=VMEM,
        cost_estimate=cost(4 * tile_flops, 2 * field_bytes),
        compiler_params=pltpu.CompilerParams(vmem_limit_bytes=32 << 20),
    )((pix_index * pixel_rows).reshape(1), fields, ref_pixels[:, None])
    early = lax.all_to_all(early, "pix", 0, 0, tiled=True)
    ref_terms = jnp.sum(early[:, 2 * diag_cols : 2 * diag_cols + 4, :].astype(F32), axis=0)
    own_ref = ref_terms.reshape(2, 2, width).sum(axis=1)
    pairs = []
    for p in range(pix_count):
        step = p // tile_dests + 1
        for m in range(mode_count):
            pairs.append((p * mode_count + (m + step) % mode_count, p * mode_count + m))
    other_ref = lax.ppermute(own_ref, ("pix", "mode"), pairs)

    first_core = mode_index % 2 == 0
    one = swap(jnp.where(first_core, two, fields))
    three = swap(jnp.where(first_core, four, two))
    band = pl.pallas_call(
        band_kernel,
        out_shape=jax.ShapeDtypeStruct((pix_count, 2 * part_cols, width), BF16),
        in_specs=[VMEM] * 5,
        out_specs=VMEM,
        cost_estimate=cost(tiles * tile_flops, 8 * field_bytes),
        compiler_params=pltpu.CompilerParams(vmem_limit_bytes=32 << 20),
    )(fields, one, two, three, four)
    band = lax.all_to_all(band, "pix", 0, 0, tiled=True)

    starts = jnp.stack([(pix_index % tile_dests) * part_cols, pix_index * diag_cols])
    scale = 1.0 / math.sqrt(pix_count * pixel_rows)
    band_out, diag_out = pl.pallas_call(
        lambda *refs: final_kernel(scale, *refs),
        out_shape=(
            jax.ShapeDtypeStruct((2, part_cols, width), F32),
            jax.ShapeDtypeStruct((2, diag_cols, width), F32),
        ),
        in_specs=[SMEM] + [VMEM] * 4,
        out_specs=(VMEM, VMEM),
        cost_estimate=cost(4 * field_bytes, 6 * field_bytes),
        compiler_params=pltpu.CompilerParams(vmem_limit_bytes=32 << 20),
    )(starts, early, own_ref, other_ref, band)
    return jnp.transpose(band_out, (0, 2, 1)), jnp.transpose(diag_out, (0, 2, 1))


def solution(mesh):
    return jax.shard_map(
        shards,
        mesh=mesh,
        in_specs=(P(None, "pix", "mode"), P()),
        out_specs=(P(None, "mode", "pix"), P(None, "mode", "pix")),
        check_vma=False,
    )
```

```python
import math

import jax
import jax.numpy as jnp
from jax import lax
from jax.experimental import pallas as pl
from jax.experimental.pallas import tpu as pltpu
from jax.sharding import PartitionSpec as P

BF16 = jnp.bfloat16
F32 = jnp.float32
VMEM = pl.BlockSpec(memory_space=pltpu.VMEM)
SMEM = pl.BlockSpec(memory_space=pltpu.SMEM)
REF_ROWS = 8


def cost(flops, nbytes):
    return pl.CostEstimate(flops=flops, bytes_accessed=nbytes, transcendentals=0)


def dot_pixels(cols, rows):
    return lax.dot_general(cols, rows, (((0,), (0,)), ((), ())), preferred_element_type=F32)


def gram_t(col_real, col_imag, row_real, row_imag, row_imag_neg):
    real = dot_pixels(col_real, row_real) + dot_pixels(col_imag, row_imag)
    imag = dot_pixels(col_imag, row_real) + dot_pixels(col_real, row_imag_neg)
    return real, imag


def fields_kernel(frames_ref, fields_ref):
    fields_ref[0] = (frames_ref[0].astype(F32) - frames_ref[2].astype(F32)).astype(BF16)
    fields_ref[1] = (frames_ref[3].astype(F32) - frames_ref[1].astype(F32)).astype(BF16)


def split_terms(real, imag):
    row = lax.broadcasted_iota(jnp.int32, real.shape, 0)
    high_real = real.astype(BF16).astype(F32)
    high_imag = imag.astype(BF16).astype(F32)
    terms = jnp.where(row == 0, high_real, real - high_real)
    terms = jnp.where(row == 2, high_imag, terms)
    terms = jnp.where(row == 3, imag - high_imag, terms)
    return jnp.where(row > 3, 0.0, terms)


def ref_terms(counts, real, imag):
    return split_terms(
        jnp.dot(counts, real, preferred_element_type=F32),
        jnp.dot(counts, imag, preferred_element_type=F32),
    )


def early_kernel(base_ref, fields_ref, pixels_ref, out_ref, counts_ref):
    dests, slot_rows, width = out_ref.shape
    diag_cols = width // dests
    real, imag = fields_ref[0], fields_ref[1]
    positions = base_ref[0] + lax.broadcasted_iota(jnp.int32, (pixels_ref.shape[0], real.shape[0]), 1)
    counts = jnp.sum((pixels_ref[...] == positions).astype(F32), axis=0, keepdims=True)
    counts = jnp.broadcast_to(counts, counts_ref.shape).astype(BF16)
    counts_ref[...] = counts
    refs = ref_terms(counts, real, imag)
    diag_real, diag_imag = gram_t(real, imag, real, imag, -imag)
    rows = jnp.concatenate(
        [diag_real, diag_imag, refs, jnp.zeros((128 - refs.shape[0], width), F32)], axis=0
    ).astype(BF16)
    slot_at = lax.broadcasted_iota(jnp.int32, (dests * slot_rows, rows.shape[0]), 0)
    source = lax.broadcasted_iota(jnp.int32, (dests * slot_rows, rows.shape[0]), 1)
    dest, slot = slot_at // slot_rows, slot_at % slot_rows
    diag_source = (slot // diag_cols) * width + dest * diag_cols + slot % diag_cols
    wanted = jnp.where(slot < 2 * diag_cols, diag_source, 2 * width + slot - 2 * diag_cols)
    pick = jnp.where(wanted == source, 1.0, 0.0).astype(BF16)
    placed = jnp.dot(pick, rows, preferred_element_type=F32)
    out_ref[...] = placed.reshape(dests, slot_rows, width).astype(BF16)


def band_kernel(core_ref, own_ref, own_swap_ref, two_ref, two_swap_ref, four_ref, four_swap_ref, early_ref, counts_ref, out_ref):
    row_real, row_imag = own_ref[0], own_ref[1]
    row_imag_neg = -row_imag
    width = row_real.shape[1]
    slot_rows = early_ref.shape[1]
    part_cols = (out_ref.shape[1] - slot_rows) // 2
    tile_dests = width // part_cols
    first_core = core_ref[0] == 0
    counts = counts_ref[...]

    def tile(at, real, imag):
        gram_real, gram_imag = gram_t(real, imag, row_real, row_imag, row_imag_neg)
        refs = ref_terms(counts, real, imag)
        dests = pl.ds(at * tile_dests, tile_dests)
        out_ref[dests, :part_cols, :] = gram_real.reshape(tile_dests, part_cols, width).astype(BF16)
        out_ref[dests, part_cols : 2 * part_cols, :] = gram_imag.reshape(tile_dests, part_cols, width).astype(BF16)
        lower = jnp.concatenate([jnp.zeros_like(refs), pltpu.roll(refs, 4, 0)], axis=0)
        early = early_ref[dests].astype(F32) + lower[None]
        out_ref[dests, 2 * part_cols :, :] = early.astype(BF16)

    def pick(a_ref, b_ref, part):
        return jnp.where(first_core, a_ref[part], b_ref[part])

    tile(0, pick(own_swap_ref, two_swap_ref, 0), pick(own_swap_ref, two_swap_ref, 1))
    tile(1, two_ref[0], two_ref[1])
    tile(2, pick(two_swap_ref, four_swap_ref, 0), pick(two_swap_ref, four_swap_ref, 1))
    tile(3, four_ref[0], four_ref[1])


def unit_phase(real, imag):
    magnitude = jnp.maximum(jnp.sqrt(real * real + imag * imag), 1.0)
    return real / magnitude, imag / magnitude


def pick_lanes(values, start, count):
    lanes = values.shape[1]
    lane = lax.broadcasted_iota(jnp.int32, (count, lanes), 1)
    row = lax.broadcasted_iota(jnp.int32, (count, lanes), 0)
    return jnp.sum(jnp.where(lane == start + row, values, 0.0), axis=1, keepdims=True)


def rotate(real, imag, row_phase, col_phase, pixel_scale):
    unit_real = row_phase[0] * col_phase[0] + row_phase[1] * col_phase[1]
    unit_imag = row_phase[1] * col_phase[0] - row_phase[0] * col_phase[1]
    return (
        (unit_real * real - unit_imag * imag) * pixel_scale,
        (unit_real * imag + unit_imag * real) * pixel_scale,
    )


def final_kernel(pixel_scale, starts_ref, parts_ref, band_out, diag_out):
    part_cols, diag_cols = band_out.shape[1], diag_out.shape[1]
    sums = jnp.sum(parts_ref[...].astype(F32), axis=0)
    band, rest = sums[: 2 * part_cols], sums[2 * part_cols :]
    diag, refs = rest[: 2 * diag_cols], rest[2 * diag_cols :]
    row_phase = unit_phase(refs[0:1] + refs[1:2], refs[2:3] + refs[3:4])
    other_phase = unit_phase(refs[4:5] + refs[5:6], refs[6:7] + refs[7:8])
    col_phase = [pick_lanes(part, starts_ref[0], part_cols) for part in other_phase]
    band_out[0], band_out[1] = rotate(band[:part_cols], band[part_cols:], row_phase, col_phase, pixel_scale)
    diag_phase = [pick_lanes(part, starts_ref[1], diag_cols) for part in row_phase]
    diag_out[0], diag_out[1] = rotate(diag[:diag_cols], diag[diag_cols:], row_phase, diag_phase, pixel_scale)


def shards(frames, ref_pixels):
    pix_count = lax.axis_size("pix")
    mode_count = lax.axis_size("mode")
    pix_index = lax.axis_index("pix")
    mode_index = lax.axis_index("mode")
    pixel_rows, width = frames.shape[1:]
    tiles = mode_count // 2
    tile_dests = pix_count // tiles
    part_cols = width // tile_dests
    diag_cols = width // pix_count
    slot_rows = 2 * diag_cols + REF_ROWS
    field_bytes = 2 * pixel_rows * width * 2
    tile_flops = 8 * pixel_rows * width * width

    def shift(array, step):
        pairs = [((m + step) % mode_count, m) for m in range(mode_count)]
        return lax.ppermute(array, "mode", pairs)

    def swap(array, even=False, odd=False):
        pairs = [(m, m ^ 1) for m in range(mode_count) if (odd if m % 2 else even)]
        return lax.ppermute(array, "mode", pairs)

    fields = pl.pallas_call(
        fields_kernel,
        out_shape=jax.ShapeDtypeStruct((2, pixel_rows, width), BF16),
        in_specs=[VMEM],
        out_specs=VMEM,
        cost_estimate=cost(4 * pixel_rows * width, 3 * field_bytes),
    )(frames)
    four = shift(fields, 4)
    two = shift(fields, 2)
    own_swap = swap(fields, odd=True)

    early, counts = pl.pallas_call(
        early_kernel,
        out_shape=(
            jax.ShapeDtypeStruct((pix_count, slot_rows, width), BF16),
            jax.ShapeDtypeStruct((8, pixel_rows), BF16),
        ),
        in_specs=[SMEM, VMEM, VMEM],
        out_specs=(VMEM, VMEM),
        cost_estimate=cost(4 * tile_flops, 2 * field_bytes),
        compiler_params=pltpu.CompilerParams(vmem_limit_bytes=32 << 20),
    )((pix_index * pixel_rows).reshape(1), fields, ref_pixels[:, None])

    two, early = lax.optimization_barrier((two, early))
    two_swap = swap(two, even=True, odd=True)
    four, early = lax.optimization_barrier((four, early))
    four_swap = swap(four, even=True)
    parts = pl.pallas_call(
        band_kernel,
        out_shape=jax.ShapeDtypeStruct((pix_count, 2 * part_cols + slot_rows, width), BF16),
        in_specs=[SMEM] + [VMEM] * 8,
        out_specs=VMEM,
        cost_estimate=cost(tiles * tile_flops, 8 * field_bytes),
        compiler_params=pltpu.CompilerParams(vmem_limit_bytes=32 << 20),
    )((mode_index % 2).reshape(1), fields, own_swap, two, two_swap, four, four_swap, early, counts)
    parts = lax.all_to_all(parts, "pix", 0, 0, tiled=True)

    starts = jnp.stack([(pix_index % tile_dests) * part_cols, pix_index * diag_cols])
    scale = 1.0 / math.sqrt(pix_count * pixel_rows)
    band_out, diag_out = pl.pallas_call(
        lambda *refs: final_kernel(scale, *refs),
        out_shape=(
            jax.ShapeDtypeStruct((2, part_cols, width), F32),
            jax.ShapeDtypeStruct((2, diag_cols, width), F32),
        ),
        in_specs=[SMEM, VMEM],
        out_specs=(VMEM, VMEM),
        cost_estimate=cost(4 * field_bytes, 6 * field_bytes),
        compiler_params=pltpu.CompilerParams(vmem_limit_bytes=32 << 20),
    )(starts, parts)
    return jnp.transpose(band_out, (0, 2, 1)), jnp.transpose(diag_out, (0, 2, 1))


def solution(mesh):
    return jax.shard_map(
        shards,
        mesh=mesh,
        in_specs=(P(None, "pix", "mode"), P()),
        out_specs=(P(None, "mode", "pix"), P(None, "mode", "pix")),
        check_vma=False,
    )
```

```python
import math

import jax
import jax.numpy as jnp
from jax import lax
from jax.experimental import pallas as pl
from jax.experimental.pallas import tpu as pltpu
from jax.sharding import Mesh
from jax.sharding import PartitionSpec as P

BF16 = jnp.bfloat16
F32 = jnp.float32
VMEM = pl.BlockSpec(memory_space=pltpu.VMEM)
SMEM = pl.BlockSpec(memory_space=pltpu.SMEM)
QUADS, NEAR = 4, 2
PIX = ("zh", "zl", "yh", "yl")


def cost(flops, nbytes):
    return pl.CostEstimate(flops=flops, bytes_accessed=nbytes, transcendentals=0)


def dot_pixels(cols, rows):
    return lax.dot_general(cols, rows, (((0,), (0,)), ((), ())), preferred_element_type=F32)


def gram_t(col_real, col_imag, row_real, row_imag, row_imag_neg):
    real = dot_pixels(col_real, row_real) + dot_pixels(col_imag, row_imag)
    imag = dot_pixels(col_imag, row_real) + dot_pixels(col_real, row_imag_neg)
    return real, imag


def fields_kernel(frames_ref, fields_ref):
    fields_ref[0] = (frames_ref[0].astype(F32) - frames_ref[2].astype(F32)).astype(BF16)
    fields_ref[1] = (frames_ref[3].astype(F32) - frames_ref[1].astype(F32)).astype(BF16)


def split_terms(real, imag):
    row = lax.broadcasted_iota(jnp.int32, real.shape, 0)
    high_real = real.astype(BF16).astype(F32)
    high_imag = imag.astype(BF16).astype(F32)
    terms = jnp.where(row == 0, high_real, real - high_real)
    terms = jnp.where(row == 2, high_imag, terms)
    terms = jnp.where(row == 3, imag - high_imag, terms)
    return jnp.where(row > 3, 0.0, terms)


def ref_terms(counts, real, imag):
    return split_terms(
        jnp.dot(counts, real, preferred_element_type=F32),
        jnp.dot(counts, imag, preferred_element_type=F32),
    )


def store_tile(out_ref, base, parts):
    width = parts[0].shape[0]
    part_cols = width // (QUADS * NEAR * NEAR)
    for zl in range(NEAR):
        for yl in range(NEAR):
            for yh in range(QUADS):
                start = ((zl * QUADS + yh) * NEAR + yl) * part_cols
                for c, part in enumerate(parts):
                    to = base + (2 * yh + c) * part_cols
                    out_ref[zl * NEAR + yl, to : to + part_cols, :] = part[start : start + part_cols].astype(BF16)


def early_kernel(base_ref, fields_ref, two_ref, pixels_ref, out_ref, counts_ref):
    near, rows, width = out_ref.shape
    real, imag = fields_ref[0], fields_ref[1]
    two_real, two_imag = two_ref[0], two_ref[1]
    positions = base_ref[0] + lax.broadcasted_iota(jnp.int32, (pixels_ref.shape[0], real.shape[0]), 1)
    counts = jnp.sum((pixels_ref[...] == positions).astype(F32), axis=0, keepdims=True)
    counts = jnp.broadcast_to(counts, counts_ref.shape).astype(BF16)
    counts_ref[...] = counts
    imag_neg = -imag
    diag = jnp.concatenate(gram_t(real, imag, real, imag, imag_neg), axis=0).astype(BF16)
    total = diag.shape[0]
    at = lax.broadcasted_iota(jnp.int32, (total, total), 0)
    source = lax.broadcasted_iota(jnp.int32, (total, total), 1)
    dests = QUADS * QUADS
    diag_cols = width // (near * dests)
    j, c = at % diag_cols, at // diag_cols % 2
    dest, neighbour = at // (2 * diag_cols) % dests, at // (2 * diag_cols * dests)
    z = dest // QUADS * NEAR + neighbour // NEAR
    y = dest % QUADS * NEAR + neighbour % NEAR
    wanted = c * width + (z * (QUADS * NEAR) + y) * diag_cols + j
    pick = jnp.where(wanted == source, 1.0, 0.0).astype(BF16)
    placed = jnp.dot(pick, diag, preferred_element_type=F32)
    share = total // near
    out_ref[:, :share, :] = placed.reshape(near, share, width).astype(BF16)
    store_tile(out_ref, share, gram_t(two_real, two_imag, real, imag, imag_neg))
    refs = ref_terms(counts, real, imag) + pltpu.roll(ref_terms(counts, two_real, two_imag), 4, 0)
    refs = jnp.concatenate([refs, jnp.zeros_like(refs)], axis=0).astype(BF16)
    out_ref[:, rows - 16 :, :] = jnp.broadcast_to(refs[None], (near, 16, width))


def band_kernel(core_ref, own_ref, own_swap_ref, two_swap_ref, four_ref, four_swap_ref, counts_ref, out_ref):
    near, rows, width = out_ref.shape
    row_real, row_imag = own_ref[0], own_ref[1]
    row_imag_neg = -row_imag
    first_core = core_ref[0] == 0
    counts = counts_ref[...]
    share = 2 * width // near

    def tile(at, real, imag):
        store_tile(out_ref, at * share, gram_t(real, imag, row_real, row_imag, row_imag_neg))
        return ref_terms(counts, real, imag)

    def pick(a_ref, b_ref, part):
        return jnp.where(first_core, a_ref[part], b_ref[part])

    one = tile(0, pick(own_swap_ref, two_swap_ref, 0), pick(own_swap_ref, two_swap_ref, 1))
    three = tile(1, pick(two_swap_ref, four_swap_ref, 0), pick(two_swap_ref, four_swap_ref, 1))
    four = tile(2, four_ref[0], four_ref[1])
    refs = jnp.concatenate([one + pltpu.roll(three, 4, 0), four], axis=0).astype(BF16)
    out_ref[:, rows - 16 :, :] = jnp.broadcast_to(refs[None], (near, 16, width))


def middle_kernel(early_ref, band_ref, out_ref):
    width = out_ref.shape[2]
    share = 2 * width // early_ref.shape[0]
    tile_rows = share // QUADS

    def total(ref, start, count):
        return jnp.sum(ref[:, start : start + count, :].astype(F32), axis=0)

    tiles = (
        total(band_ref, 0, share),
        total(early_ref, share, share),
        total(band_ref, share, share),
        total(band_ref, 2 * share, share),
    )
    early_refs = total(early_ref, 2 * share, 16)
    band_refs = total(band_ref, 3 * share, 16)
    ref_rows = (band_refs[0:4], early_refs[4:8], band_refs[4:8], band_refs[8:12])

    def again(terms):
        shape = (8, width)
        real = jnp.broadcast_to(terms[0:1] + terms[1:2], shape)
        imag = jnp.broadcast_to(terms[2:3] + terms[3:4], shape)
        return split_terms(real, imag)

    own = again(early_refs[0:4])
    diag = total(early_ref, 0, share)
    diag_rows = share // (QUADS * QUADS)
    for zh in range(QUADS):
        dests = pl.ds(zh * QUADS, QUADS)
        out_ref[dests, :tile_rows, :] = tiles[zh].reshape(QUADS, tile_rows, width).astype(BF16)
        refs = own + pltpu.roll(again(ref_rows[zh]), 4, 0)
        part = diag[zh * QUADS * diag_rows : (zh + 1) * QUADS * diag_rows].reshape(QUADS, diag_rows, width)
        rest = jnp.concatenate([part, jnp.broadcast_to(refs[None], (QUADS, 8, width))], axis=1)
        out_ref[dests, tile_rows:, :] = rest.astype(BF16)


def unit_phase(real, imag):
    magnitude = jnp.maximum(jnp.sqrt(real * real + imag * imag), 1.0)
    return real / magnitude, imag / magnitude


def pick_lanes(values, start, count):
    lanes = values.shape[1]
    lane = lax.broadcasted_iota(jnp.int32, (count, lanes), 1)
    row = lax.broadcasted_iota(jnp.int32, (count, lanes), 0)
    return jnp.sum(jnp.where(lane == start + row, values, 0.0), axis=1, keepdims=True)


def rotate(real, imag, row_phase, col_phase, pixel_scale):
    unit_real = row_phase[0] * col_phase[0] + row_phase[1] * col_phase[1]
    unit_imag = row_phase[1] * col_phase[0] - row_phase[0] * col_phase[1]
    return (
        (unit_real * real - unit_imag * imag) * pixel_scale,
        (unit_real * imag + unit_imag * real) * pixel_scale,
    )


def final_kernel(pixel_scale, starts_ref, parts_ref, band_out, diag_out):
    part_cols, diag_cols = band_out.shape[1], diag_out.shape[1]
    sums = jnp.sum(parts_ref[...].astype(F32), axis=0)
    band, rest = sums[: 2 * part_cols], sums[2 * part_cols :]
    diag, refs = rest[: 2 * diag_cols], rest[2 * diag_cols :]
    row_phase = unit_phase(refs[0:1] + refs[1:2], refs[2:3] + refs[3:4])
    other_phase = unit_phase(refs[4:5] + refs[5:6], refs[6:7] + refs[7:8])
    col_phase = [pick_lanes(part, starts_ref[0], part_cols) for part in other_phase]
    band_out[0], band_out[1] = rotate(band[:part_cols], band[part_cols:], row_phase, col_phase, pixel_scale)
    diag_phase = [pick_lanes(part, starts_ref[1], diag_cols) for part in row_phase]
    diag_out[0], diag_out[1] = rotate(diag[:diag_cols], diag[diag_cols:], row_phase, diag_phase, pixel_scale)


def shards(frames, ref_pixels):
    pix_count = lax.axis_size(PIX)
    mode_count = lax.axis_size("mode")
    pix_index = lax.axis_index(PIX)
    mode_index = lax.axis_index("mode")
    pixel_rows, width = frames.shape[1:]
    near, dests = NEAR * NEAR, QUADS * QUADS
    tile_dests = pix_count // QUADS
    part_cols = width // tile_dests
    diag_cols = width // pix_count
    share = 2 * width // near
    field_bytes = 2 * pixel_rows * width * 2
    tile_flops = 8 * pixel_rows * width * width
    params = pltpu.CompilerParams(vmem_limit_bytes=32 << 20)

    def shift(array, step):
        pairs = [((m + step) % mode_count, m) for m in range(mode_count)]
        return lax.ppermute(array, "mode", pairs)

    def swap(array, even=False, odd=False):
        pairs = [(m, m ^ 1) for m in range(mode_count) if (odd if m % 2 else even)]
        return lax.ppermute(array, "mode", pairs)

    fields = pl.pallas_call(
        fields_kernel,
        out_shape=jax.ShapeDtypeStruct((2, pixel_rows, width), BF16),
        in_specs=[VMEM],
        out_specs=VMEM,
        cost_estimate=cost(4 * pixel_rows * width, 3 * field_bytes),
    )(frames)
    two = shift(fields, 2)
    four = shift(fields, 4)
    own_swap = swap(fields, odd=True)
    two, own_swap = lax.optimization_barrier((two, own_swap))
    two_swap = swap(two, even=True, odd=True)
    early, counts = pl.pallas_call(
        early_kernel,
        out_shape=(
            jax.ShapeDtypeStruct((near, 2 * share + 16, width), BF16),
            jax.ShapeDtypeStruct((8, pixel_rows), BF16),
        ),
        in_specs=[SMEM, VMEM, VMEM, VMEM],
        out_specs=(VMEM, VMEM),
        cost_estimate=cost(2 * tile_flops, 4 * field_bytes),
        compiler_params=params,
    )((pix_index * pixel_rows).reshape(1), fields, two, ref_pixels[:, None])
    early = lax.all_to_all(early, ("zl", "yl"), 0, 0, tiled=True)
    four, two_swap, counts = lax.optimization_barrier((four, two_swap, counts))
    four_swap = swap(four, even=True)
    band = pl.pallas_call(
        band_kernel,
        out_shape=jax.ShapeDtypeStruct((near, 3 * share + 16, width), BF16),
        in_specs=[SMEM] + [VMEM] * 6,
        out_specs=VMEM,
        cost_estimate=cost(3 * tile_flops, 8 * field_bytes),
        compiler_params=params,
    )((mode_index % 2).reshape(1), fields, own_swap, two_swap, four, four_swap, counts)
    band = lax.all_to_all(band, ("zl", "yl"), 0, 0, tiled=True)
    parts = pl.pallas_call(
        middle_kernel,
        out_shape=jax.ShapeDtypeStruct((dests, 2 * part_cols + 2 * diag_cols + 8, width), BF16),
        in_specs=[VMEM, VMEM],
        out_specs=VMEM,
        cost_estimate=cost(4 * field_bytes, 4 * field_bytes),
        compiler_params=params,
    )(early, band)
    starts = jnp.stack([(pix_index % tile_dests) * part_cols, pix_index * diag_cols])
    parts, starts = lax.optimization_barrier((parts, starts))
    parts = lax.all_to_all(parts, ("zh", "yh"), 0, 0, tiled=True)

    scale = 1.0 / math.sqrt(pix_count * pixel_rows)
    band_out, diag_out = pl.pallas_call(
        lambda *refs: final_kernel(scale, *refs),
        out_shape=(
            jax.ShapeDtypeStruct((2, part_cols, width), F32),
            jax.ShapeDtypeStruct((2, diag_cols, width), F32),
        ),
        in_specs=[SMEM, VMEM],
        out_specs=(VMEM, VMEM),
        cost_estimate=cost(field_bytes, field_bytes),
        compiler_params=params,
    )(starts, parts)
    return jnp.transpose(band_out, (0, 2, 1)), jnp.transpose(diag_out, (0, 2, 1))


def solution(mesh):
    split = Mesh(mesh.devices.reshape(QUADS, NEAR, QUADS, NEAR, -1), (*PIX, "mode"))
    return jax.shard_map(
        shards,
        mesh=split,
        in_specs=(P(None, PIX, "mode"), P()),
        out_specs=(P(None, "mode", PIX), P(None, "mode", PIX)),
        check_vma=False,
    )
```

```python
import math

import jax
import jax.numpy as jnp
from jax import lax
from jax.experimental import pallas as pl
from jax.experimental.pallas import tpu as pltpu
from jax.sharding import Mesh
from jax.sharding import PartitionSpec as P

BF16 = jnp.bfloat16
F32 = jnp.float32
VMEM = pl.BlockSpec(memory_space=pltpu.VMEM)
SMEM = pl.BlockSpec(memory_space=pltpu.SMEM)
QUADS, NEAR = 4, 2
REF_ROWS = 32
PIX = ("zh", "zl", "yh", "yl")


def cost(flops, nbytes):
    return pl.CostEstimate(flops=flops, bytes_accessed=nbytes, transcendentals=0)


def dot_pixels(cols, rows):
    return lax.dot_general(cols, rows, (((0,), (0,)), ((), ())), preferred_element_type=F32)


def gram_t(col_real, col_imag, row_real, row_imag, row_imag_neg):
    real = dot_pixels(col_real, row_real) + dot_pixels(col_imag, row_imag)
    imag = dot_pixels(col_imag, row_real) + dot_pixels(col_real, row_imag_neg)
    return real, imag


def fields_kernel(frames_ref, fields_ref):
    fields_ref[0] = (frames_ref[0].astype(F32) - frames_ref[2].astype(F32)).astype(BF16)
    fields_ref[1] = (frames_ref[3].astype(F32) - frames_ref[1].astype(F32)).astype(BF16)


def split_terms(real, imag):
    row = lax.broadcasted_iota(jnp.int32, real.shape, 0)
    high_real = real.astype(BF16).astype(F32)
    high_imag = imag.astype(BF16).astype(F32)
    terms = jnp.where(row == 0, high_real, real - high_real)
    terms = jnp.where(row == 2, high_imag, terms)
    terms = jnp.where(row == 3, imag - high_imag, terms)
    return jnp.where(row > 3, 0.0, terms)


def ref_terms(counts, real, imag):
    return split_terms(
        jnp.dot(counts, real, preferred_element_type=F32),
        jnp.dot(counts, imag, preferred_element_type=F32),
    )


def store_tile(out_ref, base, parts):
    width = parts[0].shape[0]
    part_cols = width // (QUADS * NEAR * NEAR)
    for zl in range(NEAR):
        for yl in range(NEAR):
            for yh in range(QUADS):
                start = ((zl * QUADS + yh) * NEAR + yl) * part_cols
                for c, part in enumerate(parts):
                    to = base + (2 * yh + c) * part_cols
                    out_ref[zl * NEAR + yl, to : to + part_cols, :] = part[start : start + part_cols].astype(BF16)


def diag_kernel(base_ref, fields_ref, pixels_ref, out_ref, counts_ref):
    near, share, width = out_ref.shape
    real, imag = fields_ref[0], fields_ref[1]
    positions = base_ref[0] + lax.broadcasted_iota(jnp.int32, (pixels_ref.shape[0], real.shape[0]), 1)
    counts = jnp.sum((pixels_ref[...] == positions).astype(F32), axis=0, keepdims=True)
    counts_ref[...] = jnp.broadcast_to(counts, counts_ref.shape).astype(BF16)
    diag = jnp.concatenate(gram_t(real, imag, real, imag, -imag), axis=0).astype(BF16)
    total = diag.shape[0]
    at = lax.broadcasted_iota(jnp.int32, (total, total), 0)
    source = lax.broadcasted_iota(jnp.int32, (total, total), 1)
    dests = QUADS * QUADS
    diag_cols = width // (near * dests)
    j, c = at % diag_cols, at // diag_cols % 2
    dest, neighbour = at // (2 * diag_cols) % dests, at // (2 * diag_cols * dests)
    z = dest // QUADS * NEAR + neighbour // NEAR
    y = dest % QUADS * NEAR + neighbour % NEAR
    wanted = c * width + (z * (QUADS * NEAR) + y) * diag_cols + j
    pick = jnp.where(wanted == source, 1.0, 0.0).astype(BF16)
    placed = jnp.dot(pick, diag, preferred_element_type=F32)
    out_ref[...] = placed.reshape(near, share, width).astype(BF16)


def same_core_kernel(own_ref, two_ref, four_ref, out_ref):
    row_real, row_imag = own_ref[0], own_ref[1]
    row_imag_neg = -row_imag
    share = out_ref.shape[1] // 2
    store_tile(out_ref, 0, gram_t(two_ref[0], two_ref[1], row_real, row_imag, row_imag_neg))
    store_tile(out_ref, share, gram_t(four_ref[0], four_ref[1], row_real, row_imag, row_imag_neg))


def parts_kernel(
    core_ref, own_ref, own_swap_ref, two_ref, two_swap_ref, four_ref, four_swap_ref, counts_ref, diag_ref, same_ref, out_ref
):
    near, rows, width = out_ref.shape
    row_real, row_imag = own_ref[0], own_ref[1]
    row_imag_neg = -row_imag
    first_core = core_ref[0] == 0
    counts = counts_ref[...]
    share = diag_ref.shape[1]

    def pick(a_ref, b_ref, part):
        return jnp.where(first_core, a_ref[part], b_ref[part])

    one = pick(own_swap_ref, two_swap_ref, 0), pick(own_swap_ref, two_swap_ref, 1)
    three = pick(two_swap_ref, four_swap_ref, 0), pick(two_swap_ref, four_swap_ref, 1)
    store_tile(out_ref, 0, gram_t(*one, row_real, row_imag, row_imag_neg))
    store_tile(out_ref, share, gram_t(*three, row_real, row_imag, row_imag_neg))
    out_ref[:, 2 * share : 4 * share, :] = same_ref[...]
    out_ref[:, 4 * share : 5 * share, :] = diag_ref[...]
    first = ref_terms(counts, row_real, row_imag) + pltpu.roll(ref_terms(counts, *one), 4, 0)
    second = ref_terms(counts, two_ref[0], two_ref[1]) + pltpu.roll(ref_terms(counts, *three), 4, 0)
    third = ref_terms(counts, four_ref[0], four_ref[1])
    refs = jnp.concatenate([first, second, third, jnp.zeros_like(third)], axis=0).astype(BF16)
    out_ref[:, 5 * share :, :] = jnp.broadcast_to(refs[None], (near, rows - 5 * share, width))


def middle_kernel(parts_ref, out_ref):
    near, _, width = parts_ref.shape
    share = 2 * width // near
    tile_rows = share // QUADS

    def total(start, count):
        return jnp.sum(parts_ref[:, start : start + count, :].astype(F32), axis=0)

    def again(terms):
        shape = (8, width)
        real = jnp.broadcast_to(terms[0:1] + terms[1:2], shape)
        imag = jnp.broadcast_to(terms[2:3] + terms[3:4], shape)
        return split_terms(real, imag)

    refs = total(5 * share, REF_ROWS)
    own = again(refs[0:4])
    diag = total(4 * share, share)
    diag_rows = share // (QUADS * QUADS)
    for zh, at in enumerate((0, 2, 1, 3)):
        dests = pl.ds(zh * QUADS, QUADS)
        out_ref[dests, :tile_rows, :] = total(at * share, share).reshape(QUADS, tile_rows, width).astype(BF16)
        both = own + pltpu.roll(again(refs[4 * zh + 4 : 4 * zh + 8]), 4, 0)
        part = diag[zh * QUADS * diag_rows : (zh + 1) * QUADS * diag_rows].reshape(QUADS, diag_rows, width)
        rest = jnp.concatenate([part, jnp.broadcast_to(both[None], (QUADS, 8, width))], axis=1)
        out_ref[dests, tile_rows:, :] = rest.astype(BF16)


def unit_phase(real, imag):
    magnitude = jnp.maximum(jnp.sqrt(real * real + imag * imag), 1.0)
    return real / magnitude, imag / magnitude


def pick_lanes(values, start, count):
    lanes = values.shape[1]
    lane = lax.broadcasted_iota(jnp.int32, (count, lanes), 1)
    row = lax.broadcasted_iota(jnp.int32, (count, lanes), 0)
    return jnp.sum(jnp.where(lane == start + row, values, 0.0), axis=1, keepdims=True)


def rotate(real, imag, row_phase, col_phase, pixel_scale):
    unit_real = row_phase[0] * col_phase[0] + row_phase[1] * col_phase[1]
    unit_imag = row_phase[1] * col_phase[0] - row_phase[0] * col_phase[1]
    return (
        (unit_real * real - unit_imag * imag) * pixel_scale,
        (unit_real * imag + unit_imag * real) * pixel_scale,
    )


def final_kernel(pixel_scale, starts_ref, parts_ref, band_out, diag_out):
    part_cols, diag_cols = band_out.shape[1], diag_out.shape[1]
    sums = jnp.sum(parts_ref[...].astype(F32), axis=0)
    band, rest = sums[: 2 * part_cols], sums[2 * part_cols :]
    diag, refs = rest[: 2 * diag_cols], rest[2 * diag_cols :]
    row_phase = unit_phase(refs[0:1] + refs[1:2], refs[2:3] + refs[3:4])
    other_phase = unit_phase(refs[4:5] + refs[5:6], refs[6:7] + refs[7:8])
    col_phase = [pick_lanes(part, starts_ref[0], part_cols) for part in other_phase]
    band_out[0], band_out[1] = rotate(band[:part_cols], band[part_cols:], row_phase, col_phase, pixel_scale)
    diag_phase = [pick_lanes(part, starts_ref[1], diag_cols) for part in row_phase]
    diag_out[0], diag_out[1] = rotate(diag[:diag_cols], diag[diag_cols:], row_phase, diag_phase, pixel_scale)


def shards(frames, ref_pixels):
    pix_count = lax.axis_size(PIX)
    mode_count = lax.axis_size("mode")
    pix_index = lax.axis_index(PIX)
    mode_index = lax.axis_index("mode")
    pixel_rows, width = frames.shape[1:]
    near, dests = NEAR * NEAR, QUADS * QUADS
    tile_dests = pix_count // QUADS
    part_cols = width // tile_dests
    diag_cols = width // pix_count
    share = 2 * width // near
    field_bytes = 2 * pixel_rows * width * 2
    tile_flops = 8 * pixel_rows * width * width
    params = pltpu.CompilerParams(vmem_limit_bytes=32 << 20)

    def shift(array, step):
        pairs = [((m + step) % mode_count, m) for m in range(mode_count)]
        return lax.ppermute(array, "mode", pairs)

    def swap(array, even=False, odd=False):
        pairs = [(m, m ^ 1) for m in range(mode_count) if (odd if m % 2 else even)]
        return lax.ppermute(array, "mode", pairs)

    fields = pl.pallas_call(
        fields_kernel,
        out_shape=jax.ShapeDtypeStruct((2, pixel_rows, width), BF16),
        in_specs=[VMEM],
        out_specs=VMEM,
        cost_estimate=cost(4 * pixel_rows * width, 3 * field_bytes),
    )(frames)
    two = shift(fields, 2)
    four = shift(fields, 4)
    own_swap = swap(fields, odd=True)
    diag, counts = pl.pallas_call(
        diag_kernel,
        out_shape=(
            jax.ShapeDtypeStruct((near, share, width), BF16),
            jax.ShapeDtypeStruct((8, pixel_rows), BF16),
        ),
        in_specs=[SMEM, VMEM, VMEM],
        out_specs=(VMEM, VMEM),
        cost_estimate=cost(tile_flops, 2 * field_bytes),
        compiler_params=params,
    )((pix_index * pixel_rows).reshape(1), fields, ref_pixels[:, None])
    two, own_swap, diag = lax.optimization_barrier((two, own_swap, diag))
    two_swap = swap(two, even=True, odd=True)
    four, two_swap = lax.optimization_barrier((four, two_swap))
    four_swap = swap(four, even=True)
    same = pl.pallas_call(
        same_core_kernel,
        out_shape=jax.ShapeDtypeStruct((near, 2 * share, width), BF16),
        in_specs=[VMEM] * 3,
        out_specs=VMEM,
        cost_estimate=cost(2 * tile_flops, 4 * field_bytes),
        compiler_params=params,
    )(fields, two, four)
    parts = pl.pallas_call(
        parts_kernel,
        out_shape=jax.ShapeDtypeStruct((near, 5 * share + REF_ROWS, width), BF16),
        in_specs=[SMEM] + [VMEM] * 9,
        out_specs=VMEM,
        cost_estimate=cost(2 * tile_flops, 8 * field_bytes),
        compiler_params=params,
    )((mode_index % 2).reshape(1), fields, own_swap, two, two_swap, four, four_swap, counts, diag, same)
    parts = lax.all_to_all(parts, ("zl", "yl"), 0, 0, tiled=True)
    parts = pl.pallas_call(
        middle_kernel,
        out_shape=jax.ShapeDtypeStruct((dests, 2 * part_cols + 2 * diag_cols + 8, width), BF16),
        in_specs=[VMEM],
        out_specs=VMEM,
        cost_estimate=cost(4 * field_bytes, 4 * field_bytes),
        compiler_params=params,
    )(parts)
    starts = jnp.stack([(pix_index % tile_dests) * part_cols, pix_index * diag_cols])
    parts, starts = lax.optimization_barrier((parts, starts))
    parts = lax.all_to_all(parts, ("zh", "yh"), 0, 0, tiled=True)

    scale = 1.0 / math.sqrt(pix_count * pixel_rows)
    band_out, diag_out = pl.pallas_call(
        lambda *refs: final_kernel(scale, *refs),
        out_shape=(
            jax.ShapeDtypeStruct((2, part_cols, width), F32),
            jax.ShapeDtypeStruct((2, diag_cols, width), F32),
        ),
        in_specs=[SMEM, VMEM],
        out_specs=(VMEM, VMEM),
        cost_estimate=cost(field_bytes, field_bytes),
        compiler_params=params,
    )(starts, parts)
    return jnp.transpose(band_out, (0, 2, 1)), jnp.transpose(diag_out, (0, 2, 1))


def solution(mesh):
    split = Mesh(mesh.devices.reshape(QUADS, NEAR, QUADS, NEAR, -1), (*PIX, "mode"))
    return jax.shard_map(
        shards,
        mesh=split,
        in_specs=(P(None, PIX, "mode"), P()),
        out_specs=(P(None, "mode", PIX), P(None, "mode", PIX)),
        check_vma=False,
    )
```

```python
import math

import jax
import jax.numpy as jnp
from jax import lax
from jax.experimental import pallas as pl
from jax.experimental.pallas import tpu as pltpu
from jax.sharding import PartitionSpec as P

BF16 = jnp.bfloat16
F32 = jnp.float32
VMEM = pl.BlockSpec(memory_space=pltpu.VMEM)
SMEM = pl.BlockSpec(memory_space=pltpu.SMEM)
HBM = pl.BlockSpec(memory_space=pltpu.HBM)
REF_ROWS = 8


def cost(flops, nbytes):
    return pl.CostEstimate(flops=flops, bytes_accessed=nbytes, transcendentals=0)


def dot_pixels(cols, rows):
    return lax.dot_general(cols, rows, (((0,), (0,)), ((), ())), preferred_element_type=F32)


def gram_t(col_real, col_imag, row_real, row_imag, row_imag_neg):
    real = dot_pixels(col_real, row_real) + dot_pixels(col_imag, row_imag)
    imag = dot_pixels(col_imag, row_real) + dot_pixels(col_real, row_imag_neg)
    return real, imag


def fields_kernel(base_ref, frames_ref, pixels_ref, fields_ref, counts_ref, held_ref, list_ref, sems):
    chunks = sems.shape[0] - 1
    size = held_ref.shape[1] // chunks
    entries = pltpu.make_async_copy(pixels_ref, list_ref, sems.at[chunks])
    entries.start()
    copies = []
    for chunk in range(chunks):
        rows = pl.ds(chunk * size, size)
        copies.append(pltpu.make_async_copy(frames_ref.at[:, rows, :], held_ref.at[:, rows, :], sems.at[chunk]))
        copies[-1].start()
    entries.wait()
    position = base_ref[0] + lax.broadcasted_iota(jnp.int32, counts_ref.shape, 1)
    counts = jnp.zeros(counts_ref.shape, F32)
    for entry in range(list_ref.shape[0]):
        counts += jnp.where(position == list_ref[entry], 1.0, 0.0)
    counts_ref[...] = counts.astype(BF16)
    for chunk in range(chunks):
        rows = pl.ds(chunk * size, size)
        copies[chunk].wait()
        fields_ref[0, rows, :] = (held_ref[0, rows, :].astype(F32) - held_ref[2, rows, :].astype(F32)).astype(BF16)
        fields_ref[1, rows, :] = (held_ref[3, rows, :].astype(F32) - held_ref[1, rows, :].astype(F32)).astype(BF16)


def early_kernel(fields_ref, counts_ref, out_ref, held_ref, sem):
    dests, slot_rows, width = out_ref.shape
    diag_cols = width // dests
    real, imag = fields_ref[0], fields_ref[1]
    counts = counts_ref[...]
    ref_real = jnp.dot(counts, real, preferred_element_type=F32)
    ref_imag = jnp.dot(counts, imag, preferred_element_type=F32)
    row = lax.broadcasted_iota(jnp.int32, ref_real.shape, 0)
    high_real = ref_real.astype(BF16).astype(F32)
    high_imag = ref_imag.astype(BF16).astype(F32)
    refs = jnp.where(row == 0, high_real, ref_real - high_real)
    refs = jnp.where(row == 2, high_imag, refs)
    refs = jnp.where(row == 3, ref_imag - high_imag, refs)
    refs = jnp.where(row > 3, 0.0, refs)
    diag_real, diag_imag = gram_t(real, imag, real, imag, -imag)
    rows = jnp.concatenate(
        [diag_real, diag_imag, refs, jnp.zeros((128 - refs.shape[0], width), F32)], axis=0
    ).astype(BF16)
    slot_at = lax.broadcasted_iota(jnp.int32, (dests * slot_rows, rows.shape[0]), 0)
    source = lax.broadcasted_iota(jnp.int32, (dests * slot_rows, rows.shape[0]), 1)
    dest, slot = slot_at // slot_rows, slot_at % slot_rows
    diag_source = (slot // diag_cols) * width + dest * diag_cols + slot % diag_cols
    wanted = jnp.where(slot < 2 * diag_cols, diag_source, 2 * width + slot - 2 * diag_cols)
    pick = jnp.where(wanted == source, 1.0, 0.0).astype(BF16)
    placed = jnp.dot(pick, rows, preferred_element_type=F32)
    held_ref[...] = placed.reshape(dests, slot_rows, width).astype(BF16)
    copy = pltpu.make_async_copy(held_ref, out_ref, sem)
    copy.start()
    copy.wait()


def choose_kernel(core_ref, own_ref, two_ref, four_ref, _, one_ref, three_ref):
    first_core = core_ref[0] == 0

    @pl.when(first_core)
    def _():
        one_ref[...] = two_ref[...]
        three_ref[...] = four_ref[...]

    @pl.when(jnp.logical_not(first_core))
    def _():
        one_ref[...] = own_ref[...]
        three_ref[...] = two_ref[...]


def tile_pair(own_ref, blocks, out_ref, first, held_ref, sems):
    row_real, row_imag = own_ref[0], own_ref[1]
    row_imag_neg = -row_imag
    _, tile_dests, rows, width = held_ref.shape
    part_cols = rows // 2
    copies = []
    for at, block in enumerate(blocks):
        tile = gram_t(block[0], block[1], row_real, row_imag, row_imag_neg)
        for c, part in enumerate(tile):
            cut = part.reshape(tile_dests, part_cols, width).astype(BF16)
            held_ref[at, :, c * part_cols : (c + 1) * part_cols, :] = cut
        dests = pl.ds((2 * at + first) * tile_dests, tile_dests)
        copies.append(pltpu.make_async_copy(held_ref.at[at], out_ref.at[dests], sems.at[at]))
        copies[-1].start()
    for copy in copies:
        copy.wait()


def same_core_kernel(own_ref, two_ref, four_ref, out_ref, held_ref, sems):
    tile_pair(own_ref, (two_ref, four_ref), out_ref, 1, held_ref, sems)


def other_core_kernel(own_ref, one_ref, three_ref, _, out_ref, held_ref, sems):
    tile_pair(own_ref, (one_ref, three_ref), out_ref, 0, held_ref, sems)


def unit_phase(real, imag):
    magnitude = jnp.maximum(jnp.sqrt(real * real + imag * imag), 1.0)
    return real / magnitude, imag / magnitude


def pick_lanes(values, start, count):
    lanes = values.shape[1]
    lane = lax.broadcasted_iota(jnp.int32, (count, lanes), 1)
    row = lax.broadcasted_iota(jnp.int32, (count, lanes), 0)
    return jnp.sum(jnp.where(lane == start + row, values, 0.0), axis=1, keepdims=True)


def rotate(real, imag, row_phase, col_phase, pixel_scale):
    unit_real = row_phase[0] * col_phase[0] + row_phase[1] * col_phase[1]
    unit_imag = row_phase[1] * col_phase[0] - row_phase[0] * col_phase[1]
    return (
        (unit_real * real - unit_imag * imag) * pixel_scale,
        (unit_real * imag + unit_imag * real) * pixel_scale,
    )


def diag_kernel(pixel_scale, starts_ref, early_ref, diag_out, refs_out):
    diag_cols = diag_out.shape[1]
    sums = jnp.sum(early_ref[...].astype(F32), axis=0)
    diag, terms = sums[: 2 * diag_cols], sums[2 * diag_cols :]
    real, imag = terms[0:1] + terms[1:2], terms[2:3] + terms[3:4]
    refs_out[0:1, :] = real
    refs_out[1:2, :] = imag
    row_phase = unit_phase(real, imag)
    diag_phase = [pick_lanes(part, starts_ref[1], diag_cols) for part in row_phase]
    diag_out[0], diag_out[1] = rotate(diag[:diag_cols], diag[diag_cols:], row_phase, diag_phase, pixel_scale)


def final_kernel(pixel_scale, starts_ref, own_ref, other_ref, band_ref, band_out):
    part_cols = band_out.shape[1]
    band = jnp.sum(band_ref[...].astype(F32), axis=0)
    row_phase = unit_phase(own_ref[0:1, :], own_ref[1:2, :])
    other_phase = unit_phase(other_ref[0:1, :], other_ref[1:2, :])
    col_phase = [pick_lanes(part, starts_ref[0], part_cols) for part in other_phase]
    band_out[0], band_out[1] = rotate(band[:part_cols], band[part_cols:], row_phase, col_phase, pixel_scale)


def shards(frames, ref_pixels):
    pix_count = lax.axis_size("pix")
    mode_count = lax.axis_size("mode")
    pix_index = lax.axis_index("pix")
    mode_index = lax.axis_index("mode")
    pixel_rows, width = frames.shape[1:]
    tiles = mode_count // 2
    tile_dests = pix_count // tiles
    part_cols = width // tile_dests
    diag_cols = width // pix_count
    slot_rows = 2 * diag_cols + REF_ROWS
    field_bytes = 2 * pixel_rows * width * 2
    tile_flops = 8 * pixel_rows * width * width
    params = pltpu.CompilerParams(vmem_limit_bytes=32 << 20)

    def shift(array, step):
        pairs = [((m + step) % mode_count, m) for m in range(mode_count)]
        return lax.ppermute(array, "mode", pairs)

    base = (pix_index * pixel_rows).reshape(1)
    core = (mode_index % 2).reshape(1)
    starts = jnp.stack([(pix_index % tile_dests) * part_cols, pix_index * diag_cols])
    scale = 1.0 / math.sqrt(pix_count * pixel_rows)
    fields, counts = pl.pallas_call(
        fields_kernel,
        out_shape=(pltpu.VMEM((2, pixel_rows, width), BF16), pltpu.VMEM((8, pixel_rows), BF16)),
        in_specs=[SMEM, HBM, HBM],
        out_specs=(VMEM, VMEM),
        scratch_shapes=[
            pltpu.VMEM(frames.shape, BF16),
            pltpu.SMEM(ref_pixels.shape, jnp.int32),
            pltpu.SemaphoreType.DMA((5,)),
        ],
        cost_estimate=cost(4 * pixel_rows * width, 3 * field_bytes),
    )(base, frames, ref_pixels)
    two = shift(fields, 2)
    four = shift(fields, 4)
    early = pl.pallas_call(
        early_kernel,
        out_shape=jax.ShapeDtypeStruct((pix_count, slot_rows, width), BF16),
        in_specs=[VMEM, VMEM],
        out_specs=HBM,
        scratch_shapes=[pltpu.VMEM((pix_count, slot_rows, width), BF16), pltpu.SemaphoreType.DMA],
        cost_estimate=cost(4 * tile_flops, 2 * field_bytes),
        compiler_params=params,
    )(fields, counts)

    one, three = pl.pallas_call(
        choose_kernel,
        out_shape=(jax.ShapeDtypeStruct(fields.shape, BF16),) * 2,
        in_specs=[SMEM] + [VMEM] * 3 + [HBM],
        out_specs=(VMEM, VMEM),
        cost_estimate=cost(0, 4 * field_bytes),
        compiler_params=params,
    )(core, fields, two, four, early)
    early = lax.all_to_all(early, "pix", 0, 0, tiled=True)
    swap = [(m, m ^ 1) for m in range(mode_count)]
    one, three = lax.ppermute(one, "mode", swap), lax.ppermute(three, "mode", swap)
    band_shape = jax.ShapeDtypeStruct((pix_count, 2 * part_cols, width), BF16)
    scratch = [pltpu.VMEM((2, tile_dests, 2 * part_cols, width), BF16), pltpu.SemaphoreType.DMA((2,))]
    same = pl.pallas_call(
        same_core_kernel,
        out_shape=band_shape,
        in_specs=[VMEM] * 3,
        out_specs=HBM,
        scratch_shapes=scratch,
        cost_estimate=cost(2 * tile_flops, 4 * field_bytes),
        compiler_params=params,
    )(fields, two, four)
    band = pl.pallas_call(
        other_core_kernel,
        out_shape=band_shape,
        in_specs=[VMEM, VMEM, VMEM, HBM],
        out_specs=HBM,
        scratch_shapes=scratch,
        input_output_aliases={3: 0},
        cost_estimate=cost(2 * tile_flops, 4 * field_bytes),
        compiler_params=params,
    )(fields, one, three, same)
    band = lax.all_to_all(band, "pix", 0, 0, tiled=True)

    diag_out, own_ref = pl.pallas_call(
        lambda *refs: diag_kernel(scale, *refs),
        out_shape=(jax.ShapeDtypeStruct((2, diag_cols, width), F32), jax.ShapeDtypeStruct((2, width), F32)),
        in_specs=[SMEM, VMEM],
        out_specs=(VMEM, VMEM),
        cost_estimate=cost(field_bytes, field_bytes),
        compiler_params=params,
    )(starts, early)
    pairs = []
    for p in range(pix_count):
        step = p // tile_dests + 1
        for m in range(mode_count):
            pairs.append((p * mode_count + (m + step) % mode_count, p * mode_count + m))
    other_ref = lax.ppermute(own_ref, ("pix", "mode"), pairs)
    band_out = pl.pallas_call(
        lambda *refs: final_kernel(scale, *refs),
        out_shape=jax.ShapeDtypeStruct((2, part_cols, width), F32),
        in_specs=[SMEM] + [VMEM] * 3,
        out_specs=VMEM,
        cost_estimate=cost(2 * field_bytes, 2 * field_bytes),
        compiler_params=params,
    )(starts, own_ref, other_ref, band)
    return jnp.transpose(band_out, (0, 2, 1)), jnp.transpose(diag_out, (0, 2, 1))


def solution(mesh):
    return jax.shard_map(
        shards,
        mesh=mesh,
        in_specs=(P(None, "pix", "mode"), P()),
        out_specs=(P(None, "mode", "pix"), P(None, "mode", "pix")),
        check_vma=False,
    )
```

```python
import math

import jax
import jax.numpy as jnp
from jax import lax
from jax.experimental import pallas as pl
from jax.experimental.pallas import tpu as pltpu
from jax.sharding import PartitionSpec as P

BF16 = jnp.bfloat16
F32 = jnp.float32
VMEM = pl.BlockSpec(memory_space=pltpu.VMEM)
SMEM = pl.BlockSpec(memory_space=pltpu.SMEM)
HBM = pl.BlockSpec(memory_space=pltpu.HBM)


def cost(flops, nbytes):
    return pl.CostEstimate(flops=flops, bytes_accessed=nbytes, transcendentals=0)


def dot_pixels(cols, rows):
    return lax.dot_general(cols, rows, (((0,), (0,)), ((), ())), preferred_element_type=F32)


def gram_t(col_real, col_imag, row_real, row_imag, row_imag_neg):
    real = dot_pixels(col_real, row_real) + dot_pixels(col_imag, row_imag)
    imag = dot_pixels(col_imag, row_real) + dot_pixels(col_real, row_imag_neg)
    return real, imag


def fields_kernel(base_ref, frames_ref, pixels_ref, fields_ref, counts_ref, held_ref, list_ref, sems):
    chunks = sems.shape[0] - 1
    size = held_ref.shape[1] // chunks
    entries = pltpu.make_async_copy(pixels_ref, list_ref, sems.at[chunks])
    entries.start()
    copies = []
    for chunk in range(chunks):
        rows = pl.ds(chunk * size, size)
        copies.append(pltpu.make_async_copy(frames_ref.at[:, rows, :], held_ref.at[:, rows, :], sems.at[chunk]))
        copies[-1].start()
    entries.wait()
    position = base_ref[0] + lax.broadcasted_iota(jnp.int32, counts_ref.shape, 1)
    counts = jnp.zeros(counts_ref.shape, F32)
    for entry in range(list_ref.shape[0]):
        counts += jnp.where(position == list_ref[entry], 1.0, 0.0)
    counts_ref[...] = counts.astype(BF16)
    for chunk in range(chunks):
        rows = pl.ds(chunk * size, size)
        copies[chunk].wait()
        fields_ref[0, rows, :] = (held_ref[0, rows, :].astype(F32) - held_ref[2, rows, :].astype(F32)).astype(BF16)
        fields_ref[1, rows, :] = (held_ref[3, rows, :].astype(F32) - held_ref[1, rows, :].astype(F32)).astype(BF16)


def early_kernel(fields_ref, counts_ref, out_ref, held_ref, sem):
    dests, slot_rows, lanes = out_ref.shape
    real, imag = fields_ref[0], fields_ref[1]
    width = real.shape[1]
    diag_cols = width // dests
    counts = counts_ref[...]
    ref_real = jnp.dot(counts, real, preferred_element_type=F32)
    ref_imag = jnp.dot(counts, imag, preferred_element_type=F32)
    row = lax.broadcasted_iota(jnp.int32, ref_real.shape, 0)
    high_real = ref_real.astype(BF16).astype(F32)
    high_imag = ref_imag.astype(BF16).astype(F32)
    refs = jnp.where(row == 0, high_real, ref_real - high_real)
    refs = jnp.where(row == 2, high_imag, refs)
    refs = jnp.where(row == 3, ref_imag - high_imag, refs)
    refs = jnp.where(row > 3, 0.0, refs)
    half = lanes - width
    refs = refs[:, :half] + pltpu.roll(refs[:, half:], 4, 0)
    diag = jnp.concatenate(gram_t(real, imag, real, imag, -imag), axis=0).astype(BF16)
    slot_at = lax.broadcasted_iota(jnp.int32, (dests * slot_rows, diag.shape[0]), 0)
    source = lax.broadcasted_iota(jnp.int32, (dests * slot_rows, diag.shape[0]), 1)
    dest, slot = slot_at // slot_rows, slot_at % slot_rows
    wanted = (slot // diag_cols) * width + dest * diag_cols + slot % diag_cols
    pick = jnp.where(wanted == source, 1.0, 0.0).astype(BF16)
    placed = jnp.dot(pick, diag, preferred_element_type=F32)
    held_ref[:, :, :width] = placed.reshape(dests, slot_rows, width).astype(BF16)
    held_ref[:, :, width:] = jnp.broadcast_to(refs[None], (dests, slot_rows, half)).astype(BF16)
    copy = pltpu.make_async_copy(held_ref, out_ref, sem)
    copy.start()
    copy.wait()


def choose_kernel(core_ref, own_ref, four_ref, _, out_ref):
    first_core = core_ref[0] == 0

    @pl.when(first_core)
    def _():
        out_ref[...] = four_ref[...]

    @pl.when(jnp.logical_not(first_core))
    def _():
        out_ref[...] = own_ref[...]


def tile_pair(own_ref, blocks, out_ref, first, held_ref, sems):
    row_real, row_imag = own_ref[0], own_ref[1]
    row_imag_neg = -row_imag
    _, tile_dests, rows, width = held_ref.shape
    part_cols = rows // 2
    copies = []
    for at, block in enumerate(blocks):
        tile = gram_t(block[0], block[1], row_real, row_imag, row_imag_neg)
        for c, part in enumerate(tile):
            cut = part.reshape(tile_dests, part_cols, width).astype(BF16)
            held_ref[at, :, c * part_cols : (c + 1) * part_cols, :] = cut
        dests = pl.ds((2 * at + first) * tile_dests, tile_dests)
        copies.append(pltpu.make_async_copy(held_ref.at[at], out_ref.at[dests], sems.at[at]))
        copies[-1].start()
    for copy in copies:
        copy.wait()


def same_core_kernel(own_ref, two_ref, four_ref, out_ref, held_ref, sems):
    tile_pair(own_ref, (two_ref, four_ref), out_ref, 1, held_ref, sems)


def other_core_kernel(core_ref, own_ref, two_swap_ref, other_swap_ref, _, out_ref, held_ref, sems):
    first_core = core_ref[0] == 0
    one = [jnp.where(first_core, other_swap_ref[part], two_swap_ref[part]) for part in range(2)]
    three = [jnp.where(first_core, two_swap_ref[part], other_swap_ref[part]) for part in range(2)]
    tile_pair(own_ref, (one, three), out_ref, 0, held_ref, sems)


def unit_phase(real, imag):
    magnitude = jnp.maximum(jnp.sqrt(real * real + imag * imag), 1.0)
    return real / magnitude, imag / magnitude


def pick_lanes(values, start, count):
    lanes = values.shape[1]
    lane = lax.broadcasted_iota(jnp.int32, (count, lanes), 1)
    row = lax.broadcasted_iota(jnp.int32, (count, lanes), 0)
    return jnp.sum(jnp.where(lane == start + row, values, 0.0), axis=1, keepdims=True)


def rotate(real, imag, row_phase, col_phase, pixel_scale):
    unit_real = row_phase[0] * col_phase[0] + row_phase[1] * col_phase[1]
    unit_imag = row_phase[1] * col_phase[0] - row_phase[0] * col_phase[1]
    return (
        (unit_real * real - unit_imag * imag) * pixel_scale,
        (unit_real * imag + unit_imag * real) * pixel_scale,
    )


def diag_kernel(pixel_scale, starts_ref, early_ref, diag_out, refs_out):
    diag_cols = diag_out.shape[1]
    sums = jnp.sum(early_ref[...].astype(F32), axis=0)
    width = refs_out.shape[1]
    diag, terms = sums[:, :width], sums[:, width:]
    real = jnp.concatenate([terms[0:1] + terms[1:2], terms[4:5] + terms[5:6]], axis=1)
    imag = jnp.concatenate([terms[2:3] + terms[3:4], terms[6:7] + terms[7:8]], axis=1)
    refs_out[0:1, :] = real
    refs_out[1:2, :] = imag
    row_phase = unit_phase(real, imag)
    diag_phase = [pick_lanes(part, starts_ref[1], diag_cols) for part in row_phase]
    diag_out[0], diag_out[1] = rotate(diag[:diag_cols], diag[diag_cols:], row_phase, diag_phase, pixel_scale)


def final_kernel(pixel_scale, starts_ref, own_ref, other_ref, band_ref, band_out):
    part_cols = band_out.shape[1]
    band = jnp.sum(band_ref[...].astype(F32), axis=0)
    row_phase = unit_phase(own_ref[0:1, :], own_ref[1:2, :])
    other_phase = unit_phase(other_ref[0:1, :], other_ref[1:2, :])
    col_phase = [pick_lanes(part, starts_ref[0], part_cols) for part in other_phase]
    band_out[0], band_out[1] = rotate(band[:part_cols], band[part_cols:], row_phase, col_phase, pixel_scale)


def shards(frames, ref_pixels):
    pix_count = lax.axis_size("pix")
    mode_count = lax.axis_size("mode")
    pix_index = lax.axis_index("pix")
    mode_index = lax.axis_index("mode")
    pixel_rows, width = frames.shape[1:]
    tiles = mode_count // 2
    tile_dests = pix_count // tiles
    part_cols = width // tile_dests
    diag_cols = width // pix_count
    early_shape = (pix_count, 2 * diag_cols, width + width // 2)
    field_bytes = 2 * pixel_rows * width * 2
    tile_flops = 8 * pixel_rows * width * width
    params = pltpu.CompilerParams(vmem_limit_bytes=32 << 20)

    def shift(array, step):
        pairs = [((m + step) % mode_count, m) for m in range(mode_count)]
        return lax.ppermute(array, "mode", pairs)

    base = (pix_index * pixel_rows).reshape(1)
    core = (mode_index % 2).reshape(1)
    starts = jnp.stack([(pix_index % tile_dests) * part_cols, pix_index * diag_cols])
    scale = 1.0 / math.sqrt(pix_count * pixel_rows)
    fields, counts = pl.pallas_call(
        fields_kernel,
        out_shape=(pltpu.VMEM((2, pixel_rows, width), BF16), pltpu.VMEM((8, pixel_rows), BF16)),
        in_specs=[SMEM, HBM, HBM],
        out_specs=(VMEM, VMEM),
        scratch_shapes=[
            pltpu.VMEM(frames.shape, BF16),
            pltpu.SMEM(ref_pixels.shape, jnp.int32),
            pltpu.SemaphoreType.DMA((5,)),
        ],
        cost_estimate=cost(4 * pixel_rows * width, 3 * field_bytes),
    )(base, frames, ref_pixels)
    two = shift(fields, 2)
    four = shift(fields, 4)
    early = pl.pallas_call(
        early_kernel,
        out_shape=jax.ShapeDtypeStruct(early_shape, BF16),
        in_specs=[VMEM, VMEM],
        out_specs=HBM,
        scratch_shapes=[pltpu.VMEM(early_shape, BF16), pltpu.SemaphoreType.DMA],
        cost_estimate=cost(4 * tile_flops, 2 * field_bytes),
        compiler_params=params,
    )(fields, counts)

    other_swap = pl.pallas_call(
        choose_kernel,
        out_shape=jax.ShapeDtypeStruct(fields.shape, BF16),
        in_specs=[SMEM] + [VMEM] * 2 + [HBM],
        out_specs=VMEM,
        cost_estimate=cost(0, 2 * field_bytes),
        compiler_params=params,
    )(core, fields, four, early)
    early = lax.all_to_all(early, "pix", 0, 0, tiled=True)
    swap = [(m, m ^ 1) for m in range(mode_count)]
    other_swap = lax.ppermute(other_swap, "mode", swap)
    two_swap = lax.ppermute(two, "mode", swap)
    band_shape = jax.ShapeDtypeStruct((pix_count, 2 * part_cols, width), BF16)
    scratch = [pltpu.VMEM((2, tile_dests, 2 * part_cols, width), BF16), pltpu.SemaphoreType.DMA((2,))]
    same = pl.pallas_call(
        same_core_kernel,
        out_shape=band_shape,
        in_specs=[VMEM] * 3,
        out_specs=HBM,
        scratch_shapes=scratch,
        cost_estimate=cost(2 * tile_flops, 4 * field_bytes),
        compiler_params=params,
    )(fields, two, four)
    band = pl.pallas_call(
        other_core_kernel,
        out_shape=band_shape,
        in_specs=[SMEM] + [VMEM] * 3 + [HBM],
        out_specs=HBM,
        scratch_shapes=scratch,
        input_output_aliases={4: 0},
        cost_estimate=cost(2 * tile_flops, 4 * field_bytes),
        compiler_params=params,
    )(core, fields, two_swap, other_swap, same)
    band = lax.all_to_all(band, "pix", 0, 0, tiled=True)

    diag_out, own_ref = pl.pallas_call(
        lambda *refs: diag_kernel(scale, *refs),
        out_shape=(jax.ShapeDtypeStruct((2, diag_cols, width), F32), jax.ShapeDtypeStruct((2, width), F32)),
        in_specs=[SMEM, VMEM],
        out_specs=(VMEM, VMEM),
        cost_estimate=cost(field_bytes, field_bytes),
        compiler_params=params,
    )(starts, early)
    pairs = []
    for p in range(pix_count):
        step = p // tile_dests + 1
        for m in range(mode_count):
            pairs.append((p * mode_count + (m + step) % mode_count, p * mode_count + m))
    other_ref = lax.ppermute(own_ref, ("pix", "mode"), pairs)
    band_out = pl.pallas_call(
        lambda *refs: final_kernel(scale, *refs),
        out_shape=jax.ShapeDtypeStruct((2, part_cols, width), F32),
        in_specs=[SMEM] + [VMEM] * 3,
        out_specs=VMEM,
        cost_estimate=cost(2 * field_bytes, 2 * field_bytes),
        compiler_params=params,
    )(starts, own_ref, other_ref, band)
    return jnp.transpose(band_out, (0, 2, 1)), jnp.transpose(diag_out, (0, 2, 1))


def solution(mesh):
    return jax.shard_map(
        shards,
        mesh=mesh,
        in_specs=(P(None, "pix", "mode"), P()),
        out_specs=(P(None, "mode", "pix"), P(None, "mode", "pix")),
        check_vma=False,
    )
```

```python
import math

import jax
import jax.numpy as jnp
from jax import lax
from jax.experimental import pallas as pl
from jax.experimental.pallas import tpu as pltpu
from jax.sharding import Mesh
from jax.sharding import PartitionSpec as P

BF16 = jnp.bfloat16
F32 = jnp.float32
QUADS, NEAR = 4, 2
PIX = ("zh", "zl", "yh", "yl")
EXCHANGE = ("yh", "zh", "yl", "zl")
VMEM = pl.BlockSpec(memory_space=pltpu.VMEM)
SMEM = pl.BlockSpec(memory_space=pltpu.SMEM)
HBM = pl.BlockSpec(memory_space=pltpu.HBM)


def cost(flops, nbytes):
    return pl.CostEstimate(flops=flops, bytes_accessed=nbytes, transcendentals=0)


def dot_pixels(cols, rows):
    return lax.dot_general(cols, rows, (((0,), (0,)), ((), ())), preferred_element_type=F32)


def gram_t(col_real, col_imag, row_real, row_imag, row_imag_neg):
    real = dot_pixels(col_real, row_real) + dot_pixels(col_imag, row_imag)
    imag = dot_pixels(col_imag, row_real) + dot_pixels(col_real, row_imag_neg)
    return real, imag


def fields_kernel(base_ref, frames_ref, pixels_ref, fields_ref, counts_ref, held_ref, list_ref, sems):
    chunks = sems.shape[0] - 1
    size = held_ref.shape[1] // chunks
    entries = pltpu.make_async_copy(pixels_ref, list_ref, sems.at[chunks])
    entries.start()
    copies = []
    for chunk in range(chunks):
        rows = pl.ds(chunk * size, size)
        copies.append(pltpu.make_async_copy(frames_ref.at[:, rows, :], held_ref.at[:, rows, :], sems.at[chunk]))
        copies[-1].start()
    entries.wait()
    position = base_ref[0] + lax.broadcasted_iota(jnp.int32, counts_ref.shape, 1)
    counts = jnp.zeros(counts_ref.shape, F32)
    for entry in range(list_ref.shape[0]):
        counts += jnp.where(position == list_ref[entry], 1.0, 0.0)
    counts_ref[...] = counts.astype(BF16)
    for chunk in range(chunks):
        rows = pl.ds(chunk * size, size)
        copies[chunk].wait()
        fields_ref[0, rows, :] = (held_ref[0, rows, :].astype(F32) - held_ref[2, rows, :].astype(F32)).astype(BF16)
        fields_ref[1, rows, :] = (held_ref[3, rows, :].astype(F32) - held_ref[1, rows, :].astype(F32)).astype(BF16)


def early_kernel(fields_ref, counts_ref, out_ref, held_ref, sem):
    dests, slot_rows, lanes = out_ref.shape
    real, imag = fields_ref[0], fields_ref[1]
    width = real.shape[1]
    diag_cols = width // dests
    counts = counts_ref[...]
    ref_real = jnp.dot(counts, real, preferred_element_type=F32)
    ref_imag = jnp.dot(counts, imag, preferred_element_type=F32)
    row = lax.broadcasted_iota(jnp.int32, ref_real.shape, 0)
    high_real = ref_real.astype(BF16).astype(F32)
    high_imag = ref_imag.astype(BF16).astype(F32)
    refs = jnp.where(row == 0, high_real, ref_real - high_real)
    refs = jnp.where(row == 2, high_imag, refs)
    refs = jnp.where(row == 3, ref_imag - high_imag, refs)
    refs = jnp.where(row > 3, 0.0, refs)
    half = lanes - width
    refs = refs[:, :half] + pltpu.roll(refs[:, half:], 4, 0)
    diag = jnp.concatenate(gram_t(real, imag, real, imag, -imag), axis=0).astype(BF16)
    slot_at = lax.broadcasted_iota(jnp.int32, (dests * slot_rows, diag.shape[0]), 0)
    source = lax.broadcasted_iota(jnp.int32, (dests * slot_rows, diag.shape[0]), 1)
    dest, slot = slot_at // slot_rows, slot_at % slot_rows
    y = dest // (QUADS * NEAR * NEAR) * NEAR + dest // NEAR % NEAR
    z = dest // (NEAR * NEAR) % QUADS * NEAR + dest % NEAR
    wanted = (slot // diag_cols) * width + (z * (QUADS * NEAR) + y) * diag_cols + slot % diag_cols
    pick = jnp.where(wanted == source, 1.0, 0.0).astype(BF16)
    placed = jnp.dot(pick, diag, preferred_element_type=F32)
    held_ref[:, :, :width] = placed.reshape(dests, slot_rows, width).astype(BF16)
    held_ref[:, :, width:] = jnp.broadcast_to(refs[None], (dests, slot_rows, half)).astype(BF16)
    copy = pltpu.make_async_copy(held_ref, out_ref, sem)
    copy.start()
    copy.wait()


def choose_kernel(core_ref, own_ref, near_ref, _, out_ref):
    first_core = core_ref[0] == 0

    @pl.when(first_core)
    def _():
        out_ref[...] = near_ref[...]

    @pl.when(jnp.logical_not(first_core))
    def _():
        out_ref[...] = own_ref[...]


def tile_pair(own_ref, blocks, out_ref, runs, held_ref, sems):
    row_real, row_imag = own_ref[0], own_ref[1]
    row_imag_neg = -row_imag
    _, _, near, rows, _ = held_ref.shape
    part_cols = rows // 2
    copies = []
    for at, block in enumerate(blocks):
        tile = gram_t(block[0], block[1], row_real, row_imag, row_imag_neg)
        for yh in range(QUADS):
            for dest in range(near):
                yl, zl = dest // NEAR, dest % NEAR
                start = ((zl * QUADS + yh) * NEAR + yl) * part_cols
                for c, part in enumerate(tile):
                    cut = part[start : start + part_cols].astype(BF16)
                    held_ref[at, yh, dest, c * part_cols : (c + 1) * part_cols, :] = cut
        copies.append(pltpu.make_async_copy(held_ref.at[at], out_ref.at[:, runs[at]], sems.at[at]))
        copies[-1].start()
    for copy in copies:
        copy.wait()


def same_core_kernel(core_ref, own_ref, first_ref, second_ref, out_ref, held_ref, sems):
    core = core_ref[0]
    tile_pair(own_ref, (first_ref, second_ref), out_ref, (1 + 2 * core, 3 - 2 * core), held_ref, sems)


def other_core_kernel(own_ref, one_ref, three_ref, _, out_ref, held_ref, sems):
    tile_pair(own_ref, (one_ref, three_ref), out_ref, (0, 2), held_ref, sems)


def unit_phase(real, imag):
    magnitude = jnp.maximum(jnp.sqrt(real * real + imag * imag), 1.0)
    return real / magnitude, imag / magnitude


def pick_lanes(values, start, count):
    lanes = values.shape[1]
    lane = lax.broadcasted_iota(jnp.int32, (count, lanes), 1)
    row = lax.broadcasted_iota(jnp.int32, (count, lanes), 0)
    return jnp.sum(jnp.where(lane == start + row, values, 0.0), axis=1, keepdims=True)


def rotate(real, imag, row_phase, col_phase, pixel_scale):
    unit_real = row_phase[0] * col_phase[0] + row_phase[1] * col_phase[1]
    unit_imag = row_phase[1] * col_phase[0] - row_phase[0] * col_phase[1]
    return (
        (unit_real * real - unit_imag * imag) * pixel_scale,
        (unit_real * imag + unit_imag * real) * pixel_scale,
    )


def diag_kernel(pixel_scale, starts_ref, early_ref, diag_out, refs_out):
    diag_cols = diag_out.shape[1]
    sums = jnp.sum(early_ref[...].astype(F32), axis=0)
    width = refs_out.shape[1]
    diag, terms = sums[:, :width], sums[:, width:]
    real = jnp.concatenate([terms[0:1] + terms[1:2], terms[4:5] + terms[5:6]], axis=1)
    imag = jnp.concatenate([terms[2:3] + terms[3:4], terms[6:7] + terms[7:8]], axis=1)
    refs_out[0:1, :] = real
    refs_out[1:2, :] = imag
    row_phase = unit_phase(real, imag)
    diag_phase = [pick_lanes(part, starts_ref[1], diag_cols) for part in row_phase]
    diag_out[0], diag_out[1] = rotate(diag[:diag_cols], diag[diag_cols:], row_phase, diag_phase, pixel_scale)


def final_kernel(pixel_scale, starts_ref, own_ref, other_ref, band_ref, band_out):
    part_cols = band_out.shape[1]
    band = jnp.sum(band_ref[...].astype(F32), axis=0)
    row_phase = unit_phase(own_ref[0:1, :], own_ref[1:2, :])
    other_phase = unit_phase(other_ref[0:1, :], other_ref[1:2, :])
    col_phase = [pick_lanes(part, starts_ref[0], part_cols) for part in other_phase]
    band_out[0], band_out[1] = rotate(band[:part_cols], band[part_cols:], row_phase, col_phase, pixel_scale)


def shards(frames, ref_pixels):
    pix_count = lax.axis_size(PIX)
    mode_count = lax.axis_size("mode")
    pix_index = lax.axis_index(PIX)
    mode_index = lax.axis_index("mode")
    pixel_rows, width = frames.shape[1:]
    tiles = mode_count // 2
    tile_dests = pix_count // tiles
    part_cols = width // tile_dests
    diag_cols = width // pix_count
    early_shape = (pix_count, 2 * diag_cols, width + width // 2)
    field_bytes = 2 * pixel_rows * width * 2
    tile_flops = 8 * pixel_rows * width * width
    params = pltpu.CompilerParams(vmem_limit_bytes=32 << 20)

    def shift(array, even_step, odd_step):
        pairs = [((m + (odd_step if m % 2 else even_step)) % mode_count, m) for m in range(mode_count)]
        return lax.ppermute(array, "mode", pairs)

    base = (pix_index * pixel_rows).reshape(1)
    core = (mode_index % 2).reshape(1)
    starts = jnp.stack([(pix_index % tile_dests) * part_cols, pix_index * diag_cols])
    scale = 1.0 / math.sqrt(pix_count * pixel_rows)
    fields, counts = pl.pallas_call(
        fields_kernel,
        out_shape=(pltpu.VMEM((2, pixel_rows, width), BF16), pltpu.VMEM((8, pixel_rows), BF16)),
        in_specs=[SMEM, HBM, HBM],
        out_specs=(VMEM, VMEM),
        scratch_shapes=[
            pltpu.VMEM(frames.shape, BF16),
            pltpu.SMEM(ref_pixels.shape, jnp.int32),
            pltpu.SemaphoreType.DMA((5,)),
        ],
        cost_estimate=cost(4 * pixel_rows * width, 3 * field_bytes),
    )(base, frames, ref_pixels)
    first = shift(fields, 2, 4)
    second = shift(fields, 4, 2)
    early = pl.pallas_call(
        early_kernel,
        out_shape=jax.ShapeDtypeStruct(early_shape, BF16),
        in_specs=[VMEM, VMEM],
        out_specs=HBM,
        scratch_shapes=[pltpu.VMEM(early_shape, BF16), pltpu.SemaphoreType.DMA],
        cost_estimate=cost(4 * tile_flops, 2 * field_bytes),
        compiler_params=params,
    )(fields, counts)

    chosen = pl.pallas_call(
        choose_kernel,
        out_shape=jax.ShapeDtypeStruct(fields.shape, BF16),
        in_specs=[SMEM] + [VMEM] * 2 + [HBM],
        out_specs=VMEM,
        cost_estimate=cost(0, 2 * field_bytes),
        compiler_params=params,
    )(core, fields, first, early)
    early = lax.all_to_all(early, EXCHANGE, 0, 0, tiled=True)
    swap = [(m, m ^ 1) for m in range(mode_count)]
    one = lax.ppermute(chosen, "mode", swap)
    three = lax.ppermute(second, "mode", swap)
    near = NEAR * NEAR
    band_shape = jax.ShapeDtypeStruct((QUADS, tiles, near, 2 * part_cols, width), BF16)
    scratch = [pltpu.VMEM((2, QUADS, near, 2 * part_cols, width), BF16), pltpu.SemaphoreType.DMA((2,))]
    same = pl.pallas_call(
        same_core_kernel,
        out_shape=band_shape,
        in_specs=[SMEM] + [VMEM] * 3,
        out_specs=HBM,
        scratch_shapes=scratch,
        cost_estimate=cost(2 * tile_flops, 4 * field_bytes),
        compiler_params=params,
    )(core, fields, first, second)
    band = pl.pallas_call(
        other_core_kernel,
        out_shape=band_shape,
        in_specs=[VMEM] * 3 + [HBM],
        out_specs=HBM,
        scratch_shapes=scratch,
        input_output_aliases={3: 0},
        cost_estimate=cost(2 * tile_flops, 4 * field_bytes),
        compiler_params=params,
    )(fields, one, three, same)
    band = lax.all_to_all(band.reshape(pix_count, 2 * part_cols, width), EXCHANGE, 0, 0, tiled=True)

    diag_out, own_ref = pl.pallas_call(
        lambda *refs: diag_kernel(scale, *refs),
        out_shape=(jax.ShapeDtypeStruct((2, diag_cols, width), F32), jax.ShapeDtypeStruct((2, width), F32)),
        in_specs=[SMEM, VMEM],
        out_specs=(VMEM, VMEM),
        cost_estimate=cost(field_bytes, field_bytes),
        compiler_params=params,
    )(starts, early)
    pairs = []
    for p in range(pix_count):
        step = p // tile_dests + 1
        for m in range(mode_count):
            pairs.append((p * mode_count + (m + step) % mode_count, p * mode_count + m))
    other_ref = lax.ppermute(own_ref, (*PIX, "mode"), pairs)
    band_out = pl.pallas_call(
        lambda *refs: final_kernel(scale, *refs),
        out_shape=jax.ShapeDtypeStruct((2, part_cols, width), F32),
        in_specs=[SMEM] + [VMEM] * 3,
        out_specs=VMEM,
        cost_estimate=cost(2 * field_bytes, 2 * field_bytes),
        compiler_params=params,
    )(starts, own_ref, other_ref, band)
    return jnp.transpose(band_out, (0, 2, 1)), jnp.transpose(diag_out, (0, 2, 1))


def solution(mesh):
    split = Mesh(mesh.devices.reshape(QUADS, NEAR, QUADS, NEAR, -1), (*PIX, "mode"))
    return jax.shard_map(
        shards,
        mesh=split,
        in_specs=(P(None, PIX, "mode"), P()),
        out_specs=(P(None, "mode", PIX), P(None, "mode", PIX)),
        check_vma=False,
    )
```

```python
import math

import jax
import jax.numpy as jnp
from jax import lax
from jax.experimental import pallas as pl
from jax.experimental.pallas import tpu as pltpu
from jax.sharding import Mesh
from jax.sharding import PartitionSpec as P

BF16 = jnp.bfloat16
F32 = jnp.float32
QUADS, NEAR = 4, 2
PIX = ("zh", "zl", "yh", "yl")
EXCHANGE = ("yh", "zh", "yl", "zl")
VMEM = pl.BlockSpec(memory_space=pltpu.VMEM)
SMEM = pl.BlockSpec(memory_space=pltpu.SMEM)
HBM = pl.BlockSpec(memory_space=pltpu.HBM)


def cost(flops, nbytes):
    return pl.CostEstimate(flops=flops, bytes_accessed=nbytes, transcendentals=0)


def dot_pixels(cols, rows):
    return lax.dot_general(cols, rows, (((0,), (0,)), ((), ())), preferred_element_type=F32)


def gram_t(col_real, col_imag, row_real, row_imag, row_imag_neg):
    real = dot_pixels(col_real, row_real) + dot_pixels(col_imag, row_imag)
    imag = dot_pixels(col_imag, row_real) + dot_pixels(col_real, row_imag_neg)
    return real, imag


def fields_kernel(base_ref, frames_ref, pixels_ref, fields_ref, counts_ref, held_ref, list_ref, sems):
    chunks = sems.shape[0] - 1
    size = held_ref.shape[1] // chunks
    entries = pltpu.make_async_copy(pixels_ref, list_ref, sems.at[chunks])
    entries.start()
    copies = []
    for chunk in range(chunks):
        rows = pl.ds(chunk * size, size)
        copies.append(pltpu.make_async_copy(frames_ref.at[:, rows, :], held_ref.at[:, rows, :], sems.at[chunk]))
        copies[-1].start()
    entries.wait()
    position = base_ref[0] + lax.broadcasted_iota(jnp.int32, counts_ref.shape, 1)
    counts = jnp.zeros(counts_ref.shape, F32)
    for entry in range(list_ref.shape[0]):
        counts += jnp.where(position == list_ref[entry], 1.0, 0.0)
    counts_ref[...] = counts.astype(BF16)
    for chunk in range(chunks):
        rows = pl.ds(chunk * size, size)
        copies[chunk].wait()
        fields_ref[0, rows, :] = (held_ref[0, rows, :].astype(F32) - held_ref[2, rows, :].astype(F32)).astype(BF16)
        fields_ref[1, rows, :] = (held_ref[3, rows, :].astype(F32) - held_ref[1, rows, :].astype(F32)).astype(BF16)


def early_kernel(fields_ref, counts_ref, out_ref, held_ref, sem):
    dests, slot_rows, lanes = out_ref.shape
    real, imag = fields_ref[0], fields_ref[1]
    width = real.shape[1]
    diag_cols = width // dests
    counts = counts_ref[...]
    ref_real = jnp.dot(counts, real, preferred_element_type=F32)
    ref_imag = jnp.dot(counts, imag, preferred_element_type=F32)
    row = lax.broadcasted_iota(jnp.int32, ref_real.shape, 0)
    high_real = ref_real.astype(BF16).astype(F32)
    high_imag = ref_imag.astype(BF16).astype(F32)
    refs = jnp.where(row == 0, high_real, ref_real - high_real)
    refs = jnp.where(row == 2, high_imag, refs)
    refs = jnp.where(row == 3, ref_imag - high_imag, refs)
    refs = jnp.where(row > 3, 0.0, refs)
    half = lanes - width
    refs = refs[:, :half] + pltpu.roll(refs[:, half:], 4, 0)
    diag = jnp.concatenate(gram_t(real, imag, real, imag, -imag), axis=0).astype(BF16)
    slot_at = lax.broadcasted_iota(jnp.int32, (dests * slot_rows, diag.shape[0]), 0)
    source = lax.broadcasted_iota(jnp.int32, (dests * slot_rows, diag.shape[0]), 1)
    dest, slot = slot_at // slot_rows, slot_at % slot_rows
    y = dest // (QUADS * NEAR * NEAR) * NEAR + dest // NEAR % NEAR
    z = dest // (NEAR * NEAR) % QUADS * NEAR + dest % NEAR
    wanted = (slot // diag_cols) * width + (z * (QUADS * NEAR) + y) * diag_cols + slot % diag_cols
    pick = jnp.where(wanted == source, 1.0, 0.0).astype(BF16)
    placed = jnp.dot(pick, diag, preferred_element_type=F32)
    held_ref[:, :, :width] = placed.reshape(dests, slot_rows, width).astype(BF16)
    held_ref[:, :, width:] = jnp.broadcast_to(refs[None], (dests, slot_rows, half)).astype(BF16)
    copy = pltpu.make_async_copy(held_ref, out_ref, sem)
    copy.start()
    copy.wait()


def choose_kernel(core_ref, own_ref, near_ref, _, out_ref):
    first_core = core_ref[0] == 0

    @pl.when(first_core)
    def _():
        out_ref[...] = near_ref[...]

    @pl.when(jnp.logical_not(first_core))
    def _():
        out_ref[...] = own_ref[...]


def tile_pair(own_ref, blocks, out_ref, runs, held_ref, sems):
    row_real, row_imag = own_ref[0], own_ref[1]
    row_imag_neg = -row_imag
    _, _, near, rows, _ = held_ref.shape
    part_cols = rows // 2
    copies = []
    for at, block in enumerate(blocks):
        tile = gram_t(block[0], block[1], row_real, row_imag, row_imag_neg)
        for yh in range(QUADS):
            for dest in range(near):
                yl, zl = dest // NEAR, dest % NEAR
                start = ((zl * QUADS + yh) * NEAR + yl) * part_cols
                for c, part in enumerate(tile):
                    cut = part[start : start + part_cols].astype(BF16)
                    held_ref[at, yh, dest, c * part_cols : (c + 1) * part_cols, :] = cut
        copies.append(pltpu.make_async_copy(held_ref.at[at], out_ref.at[:, runs[at]], sems.at[at]))
        copies[-1].start()
    for copy in copies:
        copy.wait()


def same_core_kernel(core_ref, own_ref, first_ref, second_ref, out_ref, held_ref, sems):
    core = core_ref[0]
    tile_pair(own_ref, (first_ref, second_ref), out_ref, (1 + 2 * core, 3 - 2 * core), held_ref, sems)


def other_core_kernel(own_ref, one_ref, three_ref, _, out_ref, held_ref, sems):
    tile_pair(own_ref, (one_ref, three_ref), out_ref, (0, 2), held_ref, sems)


def unit_phase(real, imag):
    magnitude = jnp.maximum(jnp.sqrt(real * real + imag * imag), 1.0)
    return real / magnitude, imag / magnitude


def pick_lanes(values, start, count):
    lanes = values.shape[1]
    lane = lax.broadcasted_iota(jnp.int32, (count, lanes), 1)
    row = lax.broadcasted_iota(jnp.int32, (count, lanes), 0)
    return jnp.sum(jnp.where(lane == start + row, values, 0.0), axis=1, keepdims=True)


def rotate(real, imag, row_phase, col_phase, pixel_scale):
    unit_real = row_phase[0] * col_phase[0] + row_phase[1] * col_phase[1]
    unit_imag = row_phase[1] * col_phase[0] - row_phase[0] * col_phase[1]
    return (
        (unit_real * real - unit_imag * imag) * pixel_scale,
        (unit_real * imag + unit_imag * real) * pixel_scale,
    )


def diag_kernel(pixel_scale, starts_ref, early_ref, diag_out, refs_out):
    diag_cols = diag_out.shape[1]
    sums = jnp.sum(early_ref[...].astype(F32), axis=0)
    width = refs_out.shape[1]
    diag, terms = sums[:, :width], sums[:, width:]
    real = jnp.concatenate([terms[0:1] + terms[1:2], terms[4:5] + terms[5:6]], axis=1)
    imag = jnp.concatenate([terms[2:3] + terms[3:4], terms[6:7] + terms[7:8]], axis=1)
    refs_out[0:1, :] = real
    refs_out[1:2, :] = imag
    row_phase = unit_phase(real, imag)
    diag_phase = [pick_lanes(part, starts_ref[1], diag_cols) for part in row_phase]
    diag_out[0], diag_out[1] = rotate(diag[:diag_cols], diag[diag_cols:], row_phase, diag_phase, pixel_scale)


def turn_kernel(pixel_scale, starts_ref, own_ref, other_ref, turn_out):
    part_cols = turn_out.shape[1]
    row_phase = unit_phase(own_ref[0:1, :], own_ref[1:2, :])
    other_phase = unit_phase(other_ref[0:1, :], other_ref[1:2, :])
    col_phase = [pick_lanes(part, starts_ref[0], part_cols) for part in other_phase]
    turn_out[0] = (row_phase[0] * col_phase[0] + row_phase[1] * col_phase[1]) * pixel_scale
    turn_out[1] = (row_phase[1] * col_phase[0] - row_phase[0] * col_phase[1]) * pixel_scale


def final_kernel(turn_ref, band_ref, band_out):
    part_cols = band_out.shape[1]
    real = jnp.sum(band_ref[:, :part_cols, :].astype(F32), axis=0)
    imag = jnp.sum(band_ref[:, part_cols:, :].astype(F32), axis=0)
    band_out[0] = turn_ref[0] * real - turn_ref[1] * imag
    band_out[1] = turn_ref[0] * imag + turn_ref[1] * real


def shards(frames, ref_pixels):
    pix_count = lax.axis_size(PIX)
    mode_count = lax.axis_size("mode")
    pix_index = lax.axis_index(PIX)
    mode_index = lax.axis_index("mode")
    pixel_rows, width = frames.shape[1:]
    tiles = mode_count // 2
    tile_dests = pix_count // tiles
    part_cols = width // tile_dests
    diag_cols = width // pix_count
    early_shape = (pix_count, 2 * diag_cols, width + width // 2)
    field_bytes = 2 * pixel_rows * width * 2
    tile_flops = 8 * pixel_rows * width * width
    params = pltpu.CompilerParams(vmem_limit_bytes=32 << 20)

    def shift(array, even_step, odd_step):
        pairs = [((m + (odd_step if m % 2 else even_step)) % mode_count, m) for m in range(mode_count)]
        return lax.ppermute(array, "mode", pairs)

    base = (pix_index * pixel_rows).reshape(1)
    core = (mode_index % 2).reshape(1)
    starts = jnp.stack([(pix_index % tile_dests) * part_cols, pix_index * diag_cols])
    scale = 1.0 / math.sqrt(pix_count * pixel_rows)
    fields, counts = pl.pallas_call(
        fields_kernel,
        out_shape=(pltpu.VMEM((2, pixel_rows, width), BF16), pltpu.VMEM((8, pixel_rows), BF16)),
        in_specs=[SMEM, HBM, HBM],
        out_specs=(VMEM, VMEM),
        scratch_shapes=[
            pltpu.VMEM(frames.shape, BF16),
            pltpu.SMEM(ref_pixels.shape, jnp.int32),
            pltpu.SemaphoreType.DMA((5,)),
        ],
        cost_estimate=cost(4 * pixel_rows * width, 3 * field_bytes),
    )(base, frames, ref_pixels)
    first = shift(fields, 2, 4)
    second = shift(fields, 4, 2)
    early = pl.pallas_call(
        early_kernel,
        out_shape=jax.ShapeDtypeStruct(early_shape, BF16),
        in_specs=[VMEM, VMEM],
        out_specs=HBM,
        scratch_shapes=[pltpu.VMEM(early_shape, BF16), pltpu.SemaphoreType.DMA],
        cost_estimate=cost(4 * tile_flops, 2 * field_bytes),
        compiler_params=params,
    )(fields, counts)

    chosen = pl.pallas_call(
        choose_kernel,
        out_shape=jax.ShapeDtypeStruct(fields.shape, BF16),
        in_specs=[SMEM] + [VMEM] * 2 + [HBM],
        out_specs=VMEM,
        cost_estimate=cost(0, 2 * field_bytes),
        compiler_params=params,
    )(core, fields, first, early)
    early = lax.all_to_all(early, EXCHANGE, 0, 0, tiled=True)
    swap = [(m, m ^ 1) for m in range(mode_count)]
    one = lax.ppermute(chosen, "mode", swap)
    three = lax.ppermute(second, "mode", swap)
    near = NEAR * NEAR
    band_shape = jax.ShapeDtypeStruct((QUADS, tiles, near, 2 * part_cols, width), BF16)
    scratch = [pltpu.VMEM((2, QUADS, near, 2 * part_cols, width), BF16), pltpu.SemaphoreType.DMA((2,))]
    same = pl.pallas_call(
        same_core_kernel,
        out_shape=band_shape,
        in_specs=[SMEM] + [VMEM] * 3,
        out_specs=HBM,
        scratch_shapes=scratch,
        cost_estimate=cost(2 * tile_flops, 4 * field_bytes),
        compiler_params=params,
    )(core, fields, first, second)
    band = pl.pallas_call(
        other_core_kernel,
        out_shape=band_shape,
        in_specs=[VMEM] * 3 + [HBM],
        out_specs=HBM,
        scratch_shapes=scratch,
        input_output_aliases={3: 0},
        cost_estimate=cost(2 * tile_flops, 4 * field_bytes),
        compiler_params=params,
    )(fields, one, three, same)
    band = lax.all_to_all(band.reshape(pix_count, 2 * part_cols, width), EXCHANGE, 0, 0, tiled=True)

    diag_out, own_ref = pl.pallas_call(
        lambda *refs: diag_kernel(scale, *refs),
        out_shape=(jax.ShapeDtypeStruct((2, diag_cols, width), F32), jax.ShapeDtypeStruct((2, width), F32)),
        in_specs=[SMEM, VMEM],
        out_specs=(VMEM, VMEM),
        cost_estimate=cost(field_bytes, field_bytes),
        compiler_params=params,
    )(starts, early)
    pairs = []
    for p in range(pix_count):
        step = p // tile_dests + 1
        for m in range(mode_count):
            pairs.append((p * mode_count + (m + step) % mode_count, p * mode_count + m))
    other_ref = lax.ppermute(own_ref, (*PIX, "mode"), pairs)
    part_shape = jax.ShapeDtypeStruct((2, part_cols, width), F32)
    turn = pl.pallas_call(
        lambda *refs: turn_kernel(scale, *refs),
        out_shape=part_shape,
        in_specs=[SMEM, VMEM, VMEM],
        out_specs=VMEM,
        cost_estimate=cost(field_bytes, field_bytes // 8),
        compiler_params=params,
    )(starts, own_ref, other_ref)
    band_out = pl.pallas_call(
        final_kernel,
        out_shape=part_shape,
        in_specs=[VMEM, VMEM],
        out_specs=VMEM,
        cost_estimate=cost(2 * field_bytes, 2 * field_bytes),
        compiler_params=params,
    )(turn, band)
    return jnp.transpose(band_out, (0, 2, 1)), jnp.transpose(diag_out, (0, 2, 1))


def solution(mesh):
    split = Mesh(mesh.devices.reshape(QUADS, NEAR, QUADS, NEAR, -1), (*PIX, "mode"))
    return jax.shard_map(
        shards,
        mesh=split,
        in_specs=(P(None, PIX, "mode"), P()),
        out_specs=(P(None, "mode", PIX), P(None, "mode", PIX)),
        check_vma=False,
    )
```

```python
import math

import jax
import jax.numpy as jnp
from jax import lax
from jax.experimental import pallas as pl
from jax.experimental.pallas import tpu as pltpu
from jax.sharding import Mesh
from jax.sharding import PartitionSpec as P

BF16 = jnp.bfloat16
F32 = jnp.float32
QUADS, NEAR = 4, 2
PIX = ("zh", "zl", "yh", "yl")
EXCHANGE = ("yh", "zh", "yl", "zl")
VMEM = pl.BlockSpec(memory_space=pltpu.VMEM)
SMEM = pl.BlockSpec(memory_space=pltpu.SMEM)
HBM = pl.BlockSpec(memory_space=pltpu.HBM)


def cost(flops, nbytes):
    return pl.CostEstimate(flops=flops, bytes_accessed=nbytes, transcendentals=0)


def dot_pixels(cols, rows):
    return lax.dot_general(cols, rows, (((0,), (0,)), ((), ())), preferred_element_type=F32)


def gram_t(col_real, col_imag, row_real, row_imag, row_imag_neg):
    real = dot_pixels(col_real, row_real) + dot_pixels(col_imag, row_imag)
    imag = dot_pixels(col_imag, row_real) + dot_pixels(col_real, row_imag_neg)
    return real, imag


def fields_kernel(base_ref, frames_ref, pixels_ref, fields_ref, counts_ref, held_ref, list_ref, sems):
    chunks = sems.shape[0] - 1
    size = held_ref.shape[1] // chunks
    entries = pltpu.make_async_copy(pixels_ref, list_ref, sems.at[chunks])
    entries.start()
    copies = []
    for chunk in range(chunks):
        rows = pl.ds(chunk * size, size)
        copies.append(pltpu.make_async_copy(frames_ref.at[:, rows, :], held_ref.at[:, rows, :], sems.at[chunk]))
        copies[-1].start()
    entries.wait()
    position = base_ref[0] + lax.broadcasted_iota(jnp.int32, counts_ref.shape, 1)
    counts = jnp.zeros(counts_ref.shape, F32)
    for entry in range(list_ref.shape[0]):
        counts += jnp.where(position == list_ref[entry], 1.0, 0.0)
    counts_ref[...] = counts.astype(BF16)
    for chunk in range(chunks):
        rows = pl.ds(chunk * size, size)
        copies[chunk].wait()
        fields_ref[0, rows, :] = (held_ref[0, rows, :].astype(F32) - held_ref[2, rows, :].astype(F32)).astype(BF16)
        fields_ref[1, rows, :] = (held_ref[3, rows, :].astype(F32) - held_ref[1, rows, :].astype(F32)).astype(BF16)


def early_kernel(fields_ref, counts_ref, out_ref, held_ref, sem):
    dests, slot_rows, lanes = out_ref.shape
    real, imag = fields_ref[0], fields_ref[1]
    width = real.shape[1]
    diag_cols = width // dests
    counts = counts_ref[...]
    ref_real = jnp.dot(counts, real, preferred_element_type=F32)
    ref_imag = jnp.dot(counts, imag, preferred_element_type=F32)
    row = lax.broadcasted_iota(jnp.int32, ref_real.shape, 0)
    high_real = ref_real.astype(BF16).astype(F32)
    high_imag = ref_imag.astype(BF16).astype(F32)
    refs = jnp.where(row == 0, high_real, ref_real - high_real)
    refs = jnp.where(row == 2, high_imag, refs)
    refs = jnp.where(row == 3, ref_imag - high_imag, refs)
    refs = jnp.where(row > 3, 0.0, refs)
    half = lanes - width
    refs = refs[:, :half] + pltpu.roll(refs[:, half:], 4, 0)
    diag = jnp.concatenate(gram_t(real, imag, real, imag, -imag), axis=0).astype(BF16)
    slot_at = lax.broadcasted_iota(jnp.int32, (dests * slot_rows, diag.shape[0]), 0)
    source = lax.broadcasted_iota(jnp.int32, (dests * slot_rows, diag.shape[0]), 1)
    dest, slot = slot_at // slot_rows, slot_at % slot_rows
    y = dest // (QUADS * NEAR * NEAR) * NEAR + dest // NEAR % NEAR
    z = dest // (NEAR * NEAR) % QUADS * NEAR + dest % NEAR
    wanted = (slot // diag_cols) * width + (z * (QUADS * NEAR) + y) * diag_cols + slot % diag_cols
    pick = jnp.where(wanted == source, 1.0, 0.0).astype(BF16)
    placed = jnp.dot(pick, diag, preferred_element_type=F32)
    held_ref[:, :, :width] = placed.reshape(dests, slot_rows, width).astype(BF16)
    held_ref[:, :, width:] = jnp.broadcast_to(refs[None], (dests, slot_rows, half)).astype(BF16)
    copy = pltpu.make_async_copy(held_ref, out_ref, sem)
    copy.start()
    copy.wait()


def choose_kernel(core_ref, own_ref, near_ref, _, out_ref):
    first_core = core_ref[0] == 0

    @pl.when(first_core)
    def _():
        out_ref[...] = near_ref[...]

    @pl.when(jnp.logical_not(first_core))
    def _():
        out_ref[...] = own_ref[...]


def tile_pair(own_ref, blocks, out_ref, runs, held_ref, sems):
    row_real, row_imag = own_ref[0], own_ref[1]
    row_imag_neg = -row_imag
    _, _, near, rows, _ = held_ref.shape
    part_cols = rows // 2
    copies = []
    for at, block in enumerate(blocks):
        tile = gram_t(block[0], block[1], row_real, row_imag, row_imag_neg)
        for yh in range(QUADS):
            for dest in range(near):
                yl, zl = dest // NEAR, dest % NEAR
                start = ((zl * QUADS + yh) * NEAR + yl) * part_cols
                for c, part in enumerate(tile):
                    cut = part[start : start + part_cols].astype(BF16)
                    held_ref[at, yh, dest, c * part_cols : (c + 1) * part_cols, :] = cut
        copies.append(pltpu.make_async_copy(held_ref.at[at], out_ref.at[:, runs[at]], sems.at[at]))
        copies[-1].start()
    for copy in copies:
        copy.wait()


def same_core_kernel(core_ref, own_ref, first_ref, second_ref, out_ref, held_ref, sems):
    core = core_ref[0]
    tile_pair(own_ref, (first_ref, second_ref), out_ref, (1 + 2 * core, 3 - 2 * core), held_ref, sems)


def other_core_kernel(own_ref, one_ref, three_ref, _, out_ref, held_ref, sems):
    tile_pair(own_ref, (one_ref, three_ref), out_ref, (0, 2), held_ref, sems)


def unit_phase(real, imag):
    magnitude = jnp.maximum(jnp.sqrt(real * real + imag * imag), 1.0)
    return real / magnitude, imag / magnitude


def pick_lanes(values, start, count):
    lanes = values.shape[1]
    lane = lax.broadcasted_iota(jnp.int32, (count, lanes), 1)
    row = lax.broadcasted_iota(jnp.int32, (count, lanes), 0)
    return jnp.sum(jnp.where(lane == start + row, values, 0.0), axis=1, keepdims=True)


def rotate(real, imag, row_phase, col_phase, pixel_scale):
    unit_real = row_phase[0] * col_phase[0] + row_phase[1] * col_phase[1]
    unit_imag = row_phase[1] * col_phase[0] - row_phase[0] * col_phase[1]
    return (
        (unit_real * real - unit_imag * imag) * pixel_scale,
        (unit_real * imag + unit_imag * real) * pixel_scale,
    )


def diag_kernel(pixel_scale, starts_ref, early_ref, diag_out, refs_out):
    diag_cols = diag_out.shape[1]
    sums = jnp.sum(early_ref[...].astype(F32), axis=0)
    width = refs_out.shape[1]
    diag, terms = sums[:, :width], sums[:, width:]
    real = jnp.concatenate([terms[0:1] + terms[1:2], terms[4:5] + terms[5:6]], axis=1)
    imag = jnp.concatenate([terms[2:3] + terms[3:4], terms[6:7] + terms[7:8]], axis=1)
    refs_out[0:1, :] = real
    refs_out[1:2, :] = imag
    row_phase = unit_phase(real, imag)
    diag_phase = [pick_lanes(part, starts_ref[1], diag_cols) for part in row_phase]
    diag_out[0], diag_out[1] = rotate(diag[:diag_cols], diag[diag_cols:], row_phase, diag_phase, pixel_scale)


def turn_kernel(pixel_scale, starts_ref, own_ref, other_ref, turn_out):
    part_cols = turn_out.shape[1]
    row_phase = unit_phase(own_ref[0:1, :], own_ref[1:2, :])
    other_phase = unit_phase(other_ref[0:1, :], other_ref[1:2, :])
    col_phase = [pick_lanes(part, starts_ref[0], part_cols) for part in other_phase]
    turn_out[0] = (row_phase[0] * col_phase[0] + row_phase[1] * col_phase[1]) * pixel_scale
    turn_out[1] = (row_phase[1] * col_phase[0] - row_phase[0] * col_phase[1]) * pixel_scale


def final_kernel(turn_ref, band_ref, band_out):
    part_cols = band_out.shape[1]
    real = jnp.sum(band_ref[:, :part_cols, :].astype(F32), axis=0)
    imag = jnp.sum(band_ref[:, part_cols:, :].astype(F32), axis=0)
    band_out[0] = turn_ref[0] * real - turn_ref[1] * imag
    band_out[1] = turn_ref[0] * imag + turn_ref[1] * real


def shards(frames, ref_pixels):
    pix_count = lax.axis_size(PIX)
    mode_count = lax.axis_size("mode")
    pix_index = lax.axis_index(PIX)
    mode_index = lax.axis_index("mode")
    pixel_rows, width = frames.shape[1:]
    tiles = mode_count // 2
    tile_dests = pix_count // tiles
    part_cols = width // tile_dests
    diag_cols = width // pix_count
    early_shape = (pix_count, 2 * diag_cols, width + width // 2)
    field_bytes = 2 * pixel_rows * width * 2
    tile_flops = 8 * pixel_rows * width * width
    params = pltpu.CompilerParams(vmem_limit_bytes=32 << 20)

    def shift(array, even_step, odd_step):
        pairs = [((m + (odd_step if m % 2 else even_step)) % mode_count, m) for m in range(mode_count)]
        return lax.ppermute(array, "mode", pairs)

    base = (pix_index * pixel_rows).reshape(1)
    core = (mode_index % 2).reshape(1)
    starts = jnp.stack([(pix_index % tile_dests) * part_cols, pix_index * diag_cols])
    scale = 1.0 / math.sqrt(pix_count * pixel_rows)
    fields, counts = pl.pallas_call(
        fields_kernel,
        out_shape=(pltpu.VMEM((2, pixel_rows, width), BF16), pltpu.VMEM((8, pixel_rows), BF16)),
        in_specs=[SMEM, HBM, HBM],
        out_specs=(VMEM, VMEM),
        scratch_shapes=[
            pltpu.VMEM(frames.shape, BF16),
            pltpu.SMEM(ref_pixels.shape, jnp.int32),
            pltpu.SemaphoreType.DMA((3,)),
        ],
        cost_estimate=cost(4 * pixel_rows * width, 3 * field_bytes),
    )(base, frames, ref_pixels)
    first = shift(fields, 2, 4)
    second = shift(fields, 4, 2)
    early = pl.pallas_call(
        early_kernel,
        out_shape=jax.ShapeDtypeStruct(early_shape, BF16),
        in_specs=[VMEM, VMEM],
        out_specs=HBM,
        scratch_shapes=[pltpu.VMEM(early_shape, BF16), pltpu.SemaphoreType.DMA],
        cost_estimate=cost(4 * tile_flops, 2 * field_bytes),
        compiler_params=params,
    )(fields, counts)

    chosen = pl.pallas_call(
        choose_kernel,
        out_shape=jax.ShapeDtypeStruct(fields.shape, BF16),
        in_specs=[SMEM] + [VMEM] * 2 + [HBM],
        out_specs=VMEM,
        cost_estimate=cost(0, 2 * field_bytes),
        compiler_params=params,
    )(core, fields, first, early)
    early = lax.all_to_all(early, EXCHANGE, 0, 0, tiled=True)
    swap = [(m, m ^ 1) for m in range(mode_count)]
    one = lax.ppermute(chosen, "mode", swap)
    three = lax.ppermute(second, "mode", swap)
    near = NEAR * NEAR
    band_shape = jax.ShapeDtypeStruct((QUADS, tiles, near, 2 * part_cols, width), BF16)
    scratch = [pltpu.VMEM((2, QUADS, near, 2 * part_cols, width), BF16), pltpu.SemaphoreType.DMA((2,))]
    same = pl.pallas_call(
        same_core_kernel,
        out_shape=band_shape,
        in_specs=[SMEM] + [VMEM] * 3,
        out_specs=HBM,
        scratch_shapes=scratch,
        cost_estimate=cost(2 * tile_flops, 4 * field_bytes),
        compiler_params=params,
    )(core, fields, first, second)
    band = pl.pallas_call(
        other_core_kernel,
        out_shape=band_shape,
        in_specs=[VMEM] * 3 + [HBM],
        out_specs=HBM,
        scratch_shapes=scratch,
        input_output_aliases={3: 0},
        cost_estimate=cost(2 * tile_flops, 4 * field_bytes),
        compiler_params=params,
    )(fields, one, three, same)
    band = lax.all_to_all(band.reshape(pix_count, 2 * part_cols, width), EXCHANGE, 0, 0, tiled=True)

    diag_out, own_ref = pl.pallas_call(
        lambda *refs: diag_kernel(scale, *refs),
        out_shape=(jax.ShapeDtypeStruct((2, diag_cols, width), F32), jax.ShapeDtypeStruct((2, width), F32)),
        in_specs=[SMEM, VMEM],
        out_specs=(VMEM, VMEM),
        cost_estimate=cost(field_bytes, field_bytes),
        compiler_params=params,
    )(starts, early)
    pairs = []
    for p in range(pix_count):
        step = p // tile_dests + 1
        for m in range(mode_count):
            pairs.append((p * mode_count + (m + step) % mode_count, p * mode_count + m))
    other_ref = lax.ppermute(own_ref, (*PIX, "mode"), pairs)
    part_shape = jax.ShapeDtypeStruct((2, part_cols, width), F32)
    turn = pl.pallas_call(
        lambda *refs: turn_kernel(scale, *refs),
        out_shape=part_shape,
        in_specs=[SMEM, VMEM, VMEM],
        out_specs=VMEM,
        cost_estimate=cost(field_bytes, field_bytes // 8),
        compiler_params=params,
    )(starts, own_ref, other_ref)
    band_out = pl.pallas_call(
        final_kernel,
        out_shape=part_shape,
        in_specs=[VMEM, VMEM],
        out_specs=VMEM,
        cost_estimate=cost(2 * field_bytes, 2 * field_bytes),
        compiler_params=params,
    )(turn, band)
    return jnp.transpose(band_out, (0, 2, 1)), jnp.transpose(diag_out, (0, 2, 1))


def solution(mesh):
    split = Mesh(mesh.devices.reshape(QUADS, NEAR, QUADS, NEAR, -1), (*PIX, "mode"))
    return jax.shard_map(
        shards,
        mesh=split,
        in_specs=(P(None, PIX, "mode"), P()),
        out_specs=(P(None, "mode", PIX), P(None, "mode", PIX)),
        check_vma=False,
    )
```
